32 devices in a mesh: rot: 8 (over y, x, core), az: 4 (over z).
Axes of the slice: x: 2, y: 2, z: 4, core: 2. Of those that a mesh axis runs over, the one named last changes fastest.
Arguments:
- inputs: bfloat16 [16, 4, 128, 128], P('rot', None, 'az'), may hold values from -6 to 6
- pre_one: bfloat16 [16, 4, 128, 128], P('rot', None, 'az'), may hold values from -8 to 8
- pre_two: bfloat16 [16, 4, 128, 128], P('rot', None, 'az'), may hold values from -8 to 8
- cotangent: bfloat16 [16, 4, 128, 128], P('rot', None, 'az'), may hold values from -6 to 6
- filt_one: bfloat16 [16, 3, 3, 128, 128], P('rot'), may hold values from -0.046875 to 0.046875
- filt_two: bfloat16 [16, 3, 3, 128, 128], P('rot'), may hold values from -0.046875 to 0.046875
Outputs:
- input_grad: bfloat16 [16, 4, 128, 128], P('rot', None, 'az')
- filt_grad_one: float32 [16, 3, 3, 128, 128], P('rot')
- filt_grad_two: float32 [16, 3, 3, 128, 128], P('rot')
The draws below stay inside these ranges and needn't reach their ends.
All inputs are finite; a program needn't handle non-finite values.
Results may differ from the reference program's by a relative error of at most 0.018.
Values may be sent and summed in bfloat16 or wider, within the bound.
A program may use at most 64 MiB of HBM per device.

```python
import jax
import jax.numpy as jnp
from jax import lax

R = 16
C = 128
H = 4
AZ = 128


def block_scale(own_key, extent, shards, smallest, top_value):
    def one(dim, blocks):
        heights = jax.random.uniform(jax.random.fold_in(jax.random.fold_in(own_key, 6), dim), (blocks,), jnp.float32, smallest / len(shards), top_value / len(shards))
        return jnp.repeat(jnp.exp(heights), extent[dim] // blocks).reshape((-1,) + (1,) * (len(extent) - dim - 1))

    level = one(*shards[0])
    for cut in shards[1:]:
        level = level * one(*cut)
    return level


def gaussian(key, extent, scale, reach, cuts=(), kind=jnp.bfloat16):
    drawn = jax.random.normal(key, extent, jnp.float32) * scale
    if len(cuts) > 0:
        drawn = block_scale(key, extent, cuts, -0.22, 0.18) * drawn
    return jnp.clip(drawn, min=-reach, max=reach).astype(kind)


def setup_inputs(seed: int = 0) -> dict:
    key_of = jax.random.split(jax.random.key(seed), 7)
    inputs = gaussian(key_of[0], (R, H, AZ, C), 1.0, 6.0, ((0, 8), (2, 4)))
    pre_one = gaussian(key_of[1], (R, H, AZ, C), 1.5, 8.0, ((0, 8), (2, 4)))
    pre_two = gaussian(key_of[2], (R, H, AZ, C), 1.5, 8.0, ((0, 8), (2, 4)))
    cotangent = gaussian(key_of[3], (R, H, AZ, C), 1.0, 6.0, ((0, 8), (2, 4)))
    filt_one = gaussian(key_of[4], (R, 3, 3, C, C), (9 * R * C) ** -0.5, 0.046875, ((0, 8),))
    filt_two = gaussian(key_of[5], (R, 3, 3, C, C), (9 * R * C) ** -0.5, 0.046875, ((0, 8),))
    return dict(inputs=inputs, pre_one=pre_one, pre_two=pre_two, cotangent=cotangent, filt_one=filt_one, filt_two=filt_two)


def wrap_pad(field):
    widened = jnp.concatenate([field[:, :, -1:], field, field[:, :, :1]], axis=2)
    return jnp.pad(widened, ((0, 0), (1, 1), (0, 0), (0, 0)))

def slope(pre):
    widened = pre.astype(jnp.float32)
    logistic = jax.nn.sigmoid(widened)
    return logistic * (1.0 + widened * (1.0 - logistic))

def data_grad(gradient, filters):
    padded = wrap_pad(gradient.astype(jnp.float32))
    weights = filters.astype(jnp.float32)
    orient = jnp.arange(R, dtype=jnp.int32)

    def single(target):
        chosen = padded[(target - orient) % R]
        summed = jnp.zeros((H, AZ, C), jnp.float32)
        for row_tap in range(3):
            for col_tap in range(3):
                window = chosen[:, 2 - row_tap:2 - row_tap + H, 2 - col_tap:2 - col_tap + AZ, :]
                summed = summed + jnp.einsum('ryxc,ric->yxi', window, weights[:, row_tap, col_tap], precision=lax.Precision.HIGHEST)
        return summed
    return lax.map(single, orient)

def weight_grad(features, gradient):
    padded = wrap_pad(features.astype(jnp.float32))
    widened = gradient.astype(jnp.float32)
    orient = jnp.arange(R, dtype=jnp.int32)

    def single(relative):
        shifted = padded[(orient + relative) % R]
        pieces = []
        for row_tap in range(3):
            for col_tap in range(3):
                window = shifted[:, row_tap:row_tap + H, col_tap:col_tap + AZ, :]
                pieces.append(jnp.einsum('gyxi,gyxo->io', window, widened, precision=lax.Precision.HIGHEST))
        return jnp.stack(pieces).reshape(3, 3, C, C)
    return lax.map(single, orient)

def reference(inputs, pre_one, pre_two, cotangent, filt_one, filt_two):
    scale = (R * H * AZ) ** (-0.5)
    act_one = jax.nn.silu(pre_one.astype(jnp.float32)).astype(jnp.bfloat16)
    grad_two = (cotangent.astype(jnp.float32) * slope(pre_two)).astype(jnp.bfloat16)
    filt_grad_two = weight_grad(act_one, grad_two) * scale
    delta_one = data_grad(grad_two, filt_two)
    grad_one = (delta_one * slope(pre_one)).astype(jnp.bfloat16)
    input_grad = data_grad(grad_one, filt_one).astype(jnp.bfloat16)
    filt_grad_one = weight_grad(inputs, grad_one) * scale
    return (input_grad, filt_grad_one, filt_grad_two)
```

```python
import functools

import jax
import jax.numpy as jnp
from jax import lax
from jax.experimental import pallas as pl
from jax.experimental.pallas import tpu as pltpu
from jax.sharding import PartitionSpec as P

F32 = jnp.float32
BF16 = jnp.bfloat16


def slope(v):
    s = jax.nn.sigmoid(v)
    return s * (1.0 + v * (1.0 - s))


def kernel(
    n, m, p, H, X, C, scale,
    inputs, pre_one, pre_two, cot, filt_one, filt_two,
    out_in, out_f1, out_f2,
    st_g, st_e, st_a, grads, edges, feats, weights, gx, lhs, outs,
    part_s, part_x, part_m, part_r, zs, zr, zt, zf,
    col_in, st_t, whole_in, whole_g, acc, turn,
    g_ss, g_rs, gf_ss, gf_rs, e_ss, e_rs, ef_ss, ef_rs, a_ss, a_rs, af_ss, af_rs,
    x_ss, x_rs, p_ss, p_rs, z_ss, z_rs, y_ss, y_rs,
    w_sem, iz_ss, iz_rs, gz_ss, gz_rs, h_ss, h_rs, hf_ss, hf_rs,
):
    R = n * p
    HX = H * X
    nc = n // 2
    K = 9 * p
    AZ = m * X
    span = p * H * AZ
    me = lax.axis_index("rot")
    z = lax.axis_index("az")
    core = lax.rem(me, 2)
    chip = lax.div(me, 2)
    sib = me + 1 - 2 * core

    def to(t):
        return 2 * lax.rem(chip + t, nc) + core

    def frm(t):
        return 2 * lax.rem(chip + nc - t, nc) + core

    def col(d):
        return lax.rem(z + d, m)

    def col_at(zz):
        return pl.ds(pl.multiple_of(zz * X, X), X)

    def g_at(owner, target_chip):
        return pl.ds(p * lax.rem(owner - 2 * target_chip + n, n), p)

    def a_at(owner, target):
        slot = lax.rem(owner - 2 * lax.div(target, 2) - target + 2 * n, n)
        return pl.ds(pl.multiple_of(slot * span, span), span)

    def copy(src, dst, ss, rs, rot, az):
        return pltpu.make_async_remote_copy(
            src_ref=src, dst_ref=dst, send_sem=ss, recv_sem=rs,
            device_id={"rot": rot, "az": az}, device_id_type=pl.DeviceIdType.MESH,
        )

    loads = [
        [
            pltpu.make_async_copy(
                filt.at[s, i, j],
                weights.at[l, pl.ds(s * C, C), pl.ds((i * 3 + j) * C, C)],
                w_sem.at[l, (s * 3 + i) * 3 + j],
            )
            for s in range(p) for i in range(3) for j in range(3)
        ]
        for l, filt in enumerate((filt_two, filt_one))
    ]
    for load in loads[0] + loads[1]:
        load.start()

    barrier = pltpu.get_barrier_semaphore()
    near_cols = sorted({1 % m, (m - 1) % m})
    partners = [(sib, z)] + [(to(t), z) for t in range(1, nc)]
    partners += [(to(t), col(d)) for d in near_cols for t in range(nc)]
    partners += [(me, col(d)) for d in range(1, m) if d not in near_cols]
    for rot, az in partners:
        pl.semaphore_signal(
            barrier, inc=1, device_id={"rot": rot, "az": az},
            device_id_type=pl.DeviceIdType.MESH,
        )

    pending = []

    def start(c):
        c.start()
        pending.append(c)
        return c

    def stage_grad(ph, value):
        st_g[ph] = value.astype(BF16)
        if ph == 0:
            grads[me] = value.astype(BF16)
        else:
            whole_g[g_at(me, chip), :, col_at(z), :] = value.astype(BF16)
        st_e[ph, 0] = value[:, :, 0, :].reshape(p * H, C).astype(BF16)
        st_e[ph, 1] = value[:, :, X - 1, :].reshape(p * H, C).astype(BF16)

    def home(ph, owner, target_chip, zz):
        if ph == 0:
            return grads.at[owner]
        return whole_g.at[g_at(owner, target_chip), :, col_at(zz), :]

    def there(t):
        return lax.rem(chip + t, nc)

    def send_grad(ph):
        rims = []
        for t in range(nc):
            for side, d in ((1, 1), (0, m - 1)):
                rims.append(
                    start(
                        copy(
                            st_e.at[ph, side], edges.at[ph, me, 1 - side],
                            e_ss.at[ph, side, t], e_rs.at[ph, side, t], to(t), col(d),
                        )
                    )
                )
        direct = [None] + [
            start(copy(st_g.at[ph], home(ph, me, there(t), z), g_ss.at[ph, t], g_rs.at[ph, t], to(t), z))
            for t in range(1, nc)
        ]
        own = start(copy(st_g.at[ph], home(ph, me, chip, z), gf_ss.at[ph, 0], gf_rs.at[ph, 0], sib, z))
        return direct, own, rims

    def relay_grad(ph, sent):
        direct, own, rims = sent
        passed = [own]
        for t in range(nc):
            rims[2 * t].wait_recv()
            rims[2 * t + 1].wait_recv()
            d = frm(t)
            passed.append(
                start(copy(edges.at[ph, d], edges.at[ph, d], ef_ss.at[ph, t], ef_rs.at[ph, t], sib, z))
            )
        for t in range(1, nc):
            direct[t].wait_recv()
            d = frm(t)
            passed.append(
                start(copy(home(ph, d, chip, z), home(ph, d, chip, z), gf_ss.at[ph, t], gf_rs.at[ph, t], sib, z))
            )
        return passed

    def stage_feat(value):
        for o in range(p):
            turned = value[o].T.astype(BF16)
            st_a[o] = turned
            feats[me, o] = turned

    def send_feat():
        direct = [None] + [
            start(copy(st_a, feats.at[me], a_ss.at[0, t], a_rs.at[0, t], to(t), z))
            for t in range(1, nc)
        ]
        own = start(copy(st_a, feats.at[me], af_ss.at[0, 0], af_rs.at[0, 0], sib, z))
        return direct, own

    def relay_feat(sent):
        direct, own = sent
        passed = [own]
        for t in range(1, nc):
            direct[t].wait_recv()
            d = frm(t)
            passed.append(
                start(copy(feats.at[d], feats.at[d], af_ss.at[0, t], af_rs.at[0, t], sib, z))
            )
        return passed

    def send_cols():
        return [None] + [
            start(copy(inputs, col_in.at[:, :, col_at(z), :], iz_ss.at[d], iz_rs.at[d], me, col(d)))
            for d in range(1, m)
        ]

    def turn_cols():
        for o in range(p):
            for y in range(H):
                st_t[:, (o * H + y) * AZ : (o * H + y + 1) * AZ] = col_in[o, y].astype(F32).T.astype(BF16)
        whole_in[C : 2 * C, a_at(me, me)] = st_t[...]

    def mid(owner, target):
        return whole_in.at[pl.ds(C, C), a_at(owner, target)]

    def send_turned():
        direct = [None] + [
            start(copy(st_t, mid(me, to(t)), a_ss.at[1, t], a_rs.at[1, t], to(t), z))
            for t in range(1, nc)
        ]
        own = start(copy(st_t, mid(me, sib), af_ss.at[1, 0], af_rs.at[1, 0], sib, z))
        return direct, own

    def relay_turned(sent):
        direct, own = sent
        passed = [own]
        for t in range(1, nc):
            direct[t].wait_recv()
            d = frm(t)
            passed.append(
                start(copy(mid(d, me), mid(d, sib), af_ss.at[1, t], af_rs.at[1, t], sib, z))
            )
        return passed

    def roll_cols(first, last):
        def body(b, carry):
            at = pl.ds(pl.multiple_of(b * AZ, AZ), AZ)
            a = whole_in[C : 2 * C, at].astype(F32)
            whole_in[0:C, at] = pltpu.roll(a, 1, 1).astype(BF16)
            whole_in[2 * C : 3 * C, at] = pltpu.roll(a, AZ - 1, 1).astype(BF16)
            return carry

        lax.fori_loop(first, last, body, 0)

    def send_grad_cols():
        return [None] + [
            start(copy(st_g.at[1], home(1, me, chip, z), gz_ss.at[d], gz_rs.at[d], me, col(d)))
            for d in range(1, m)
        ]

    def spread_grad_cols(sent):
        forwards = []
        for k in range(1, m):
            sent[k].wait_recv()
            zz = col(m - k)
            here = home(1, me, chip, zz)
            passed = [start(copy(here, here, hf_ss.at[k, 0], hf_rs.at[k, 0], sib, z))]
            direct = [
                start(copy(here, home(1, me, there(t), zz), h_ss.at[k, t], h_rs.at[k, t], to(t), z))
                for t in range(1, nc)
            ]
            forwards.append((zz, passed, [None] + direct))
        return forwards

    def relay_grad_cols(forwards, ts):
        for k, (zz, passed, direct) in enumerate(forwards, 1):
            for t in ts:
                direct[t].wait_recv()
                here = home(1, frm(t), chip, zz)
                passed.append(start(copy(here, here, hf_ss.at[k, t], hf_rs.at[k, t], sib, z)))

    def group_terms(t, first, last):
        vs = list(range(2 * p * t, 2 * p * (t + 1)))
        if t == 0:
            vs = vs[p - 1 :]
        if last:
            vs = vs + list(range(p - 1))
        for i in range(3):
            low, high = max(0, i - 1), min(H, H + i - 1)
            left = jnp.concatenate(
                [whole_in[:, (v * H + low) * AZ : (v * H + high) * AZ] for v in vs], axis=1
            )
            count = (high - low) * AZ
            right = jnp.concatenate(
                [
                    jnp.concatenate(
                        [
                            whole_g[(v - s) % R, low + 1 - i : high + 1 - i].reshape(count, C)
                            for v in vs
                        ],
                        axis=0,
                    )
                    for s in range(p)
                ],
                axis=1,
            )
            got = jnp.dot(left, right, preferred_element_type=F32)
            if not first:
                got = got + acc[i]
            if not last:
                acc[i] = got
            else:
                for s in range(p):
                    for j in range(3):
                        out_f1[s, i, j] = got[j * C : (j + 1) * C, s * C : (s + 1) * C] * scale

    def arrive(copies):
        for c in copies:
            c.wait_recv()

    def build_gx(ph):
        x_of = lax.broadcasted_iota(jnp.int32, (p * H, X, C), 1).reshape(p * HX, C)

        def body(d, carry):
            g = grads[d] if ph == 0 else whole_g[g_at(d, chip), :, col_at(z), :]
            g = g.astype(F32).reshape(p * HX, C)
            low = edges[ph, d, 0].astype(F32)
            high = edges[ph, d, 1].astype(F32)
            low = jnp.broadcast_to(low[:, None, :], (p * H, X, C)).reshape(p * HX, C)
            high = jnp.broadcast_to(high[:, None, :], (p * H, X, C)).reshape(p * HX, C)
            before = jnp.where(x_of == 0, low, pltpu.roll(g, 1, 0))
            after = jnp.where(x_of == X - 1, high, pltpu.roll(g, p * HX - 1, 0))
            for j, v in enumerate((after, g, before)):
                gx[pl.ds(d * p, p), 1 : H + 1, :, j * C : (j + 1) * C] = v.astype(BF16).reshape(p, H, X, C)
            return carry

        lax.fori_loop(0, n, body, 0)

    def build_lhs():
        lane = lax.broadcasted_iota(jnp.int32, (C, HX), 1)
        for q in range(n):
            owner = lax.rem(me + q, n)
            for o in range(p):
                block = q * p + o
                a = feats[owner, o]
                wide = a.astype(F32)
                down = jnp.where(lane < X, 0.0, pltpu.roll(wide, X, 1)).astype(BF16)
                up = jnp.where(lane >= HX - X, 0.0, pltpu.roll(wide, HX - X, 1)).astype(BF16)
                spots = [block] + ([R + block] if block < p - 1 else [])
                for spot in spots:
                    for i, v in enumerate((down, a, up)):
                        lhs[i * C : (i + 1) * C, spot * HX : (spot + 1) * HX] = v

    def term(q, o):
        total = None
        for s in range(p):
            one = outs[(q * p + o - s) % R, :, s * C : (s + 1) * C]
            total = one if total is None else total + one
        return total

    def data_terms(ph):
        for load in loads[ph]:
            load.wait()
        w = weights[ph]
        crossed = [None] * n

        def emit(q):
            for o in range(p):
                part_s[ph, q, o] = term(q, o).astype(BF16)
            t = lax.rem(q // 2 + core, nc)
            crossed[q] = start(
                copy(part_s.at[ph, q], part_x.at[ph, t], x_ss.at[ph, t], x_rs.at[ph, t], sib, z)
            )

        for q in range(n):
            rows = jnp.concatenate(
                [gx[q * p : (q + 1) * p, 2 - i : 2 - i + H].reshape(p * HX, 3 * C) for i in range(3)],
                axis=1,
            )
            got = lax.dot_general(rows, w, (((1,), (1,)), ((), ())), preferred_element_type=F32)
            outs[q * p : (q + 1) * p] = got.reshape(p, HX, p * C)
            if q % 2 == 1:
                emit(q)

    def merge_terms(ph):
        sent = []
        for t in list(range(1, nc)) + [0]:
            pltpu.make_async_remote_copy(
                src_ref=part_x.at[ph, t], dst_ref=part_x.at[ph, t],
                send_sem=x_ss.at[ph, t], recv_sem=x_rs.at[ph, t],
                device_id={"rot": sib, "az": z}, device_id_type=pl.DeviceIdType.MESH,
            ).wait_recv()
            for o in range(p):
                total = term(2 * t, o) + part_x[ph, t, o].astype(F32)
                if t == 0:
                    part_r[ph, 0, o] = total.astype(BF16)
                else:
                    part_m[ph, t, o] = total.astype(BF16)
            if t > 0:
                sent.append(
                    start(
                        copy(part_m.at[ph, t], part_r.at[ph, t], p_ss.at[ph, t], p_rs.at[ph, t], to(t), z)
                    )
                )
        return sent

    def part_sum(ph, copies):
        arrive(copies)
        total = part_r[ph, 0].astype(F32)
        for t in range(1, nc):
            total = total + part_r[ph, t].astype(F32)
        return total

    lower = z < m // 2
    near_pos = jnp.where(lower, z, m - 1 - z)
    right, left = jnp.minimum(z + 1, m - 1), jnp.maximum(z - 1, 0)
    inner = jnp.where(lower, right, left)
    outer = jnp.where(lower, left, right)
    at_end = near_pos == 0
    at_mid = near_pos == m // 2 - 1
    slot = jnp.where(at_mid, 1, 0)

    def inward(src, k):
        return copy(src, zr.at[slot, k], z_ss.at[k], z_rs.at[slot, k], me, inner)

    def crossed_in(w, k):
        return copy(zr.at[w, k], zr.at[w, k], z_ss.at[k], z_rs.at[w, k], me, inner)

    def outward(k):
        return copy(zf.at[k], zf.at[k], y_ss.at[k], y_rs.at[k], me, outer)

    def filt_terms():
        right_side = gx[:, 1 : H + 1].reshape(R * HX, 3 * C)
        for s in range(p):
            got = jnp.dot(
                lhs[:, s * HX : (s + R) * HX], right_side, preferred_element_type=F32
            )
            for i in range(3):
                for j in range(3):
                    zs[(s * 3 + i) * 3 + j] = got[i * C : (i + 1) * C, j * C : (j + 1) * C].astype(BF16)
            begin(s * 18 // p, (s + 1) * 18 // p)

    def begin(a, b):
        @pl.when(at_end)
        def _():
            for k in range(K * a // 18, K * b // 18):
                inward(zs.at[k], k).start()

    def go_in(a, b):
        @pl.when(jnp.logical_not(at_end))
        def _():
            for k in range(K * a // 18, K * b // 18):
                crossed_in(0, k).wait_recv()
                zt[k] = (zs[k].astype(F32) + zr[0, k].astype(F32)).astype(BF16)
                inward(zt.at[k], k).start()

    base = zs if m == 2 else zt

    def go_out(a, b):
        for k in range(K * a // 18, K * b // 18):

            @pl.when(at_mid)
            def _():
                crossed_in(1, k).wait_recv()
                zf[k] = (base[k].astype(F32) + zr[1, k].astype(F32)).astype(BF16)

            @pl.when(jnp.logical_not(at_mid))
            def _():
                outward(k).wait_recv()

            @pl.when(jnp.logical_not(at_end))
            def _():
                outward(k).start()

            out_f2[k // 9, k // 3 % 3, k % 3] = zf[k].astype(F32) * scale

    def drain():
        for k in range(K):
            crossed_in(0, k).wait_send()

        @pl.when(jnp.logical_not(at_end))
        def _():
            for k in range(K):
                outward(k).wait_send()

    grad_two = (cot[...].astype(F32) * slope(pre_two[...].astype(F32))).astype(BF16).astype(F32)
    stage_grad(0, grad_two)
    col_in[:, :, col_at(z), :] = inputs[...]
    wide_one = pre_one[...].astype(F32)
    stage_feat((wide_one * jax.nn.sigmoid(wide_one)).reshape(p, HX, C))
    turn[...] = slope(wide_one)
    gx[:, 0] = jnp.zeros((R, X, 3 * C), BF16)
    gx[:, H + 1] = jnp.zeros((R, X, 3 * C), BF16)
    pl.semaphore_wait(barrier, len(partners))
    g_sent = send_grad(0)
    c_sent = send_cols()
    a_sent = send_feat()
    arrive(relay_grad(0, g_sent))
    build_gx(0)
    arrive(c_sent[1:])
    turn_cols()
    i_sent = send_turned()
    a_passed = relay_feat(a_sent)
    data_terms(0)
    p_sent = merge_terms(0)
    arrive(a_passed)
    build_lhs()
    filt_terms()

    delta = part_sum(0, p_sent).reshape(p, H, X, C)
    grad_one = (delta * turn[...]).astype(BF16).astype(F32)
    stage_grad(1, grad_one)
    g_sent = send_grad(1)
    z_sent = send_grad_cols()
    i_passed = relay_turned(i_sent)
    go_in(0, 2)
    arrive(i_passed)
    roll_cols(0, R * H)
    forwards = spread_grad_cols(z_sent)
    g_passed = relay_grad(1, g_sent)
    go_in(2, 6)
    arrive(g_passed)
    build_gx(1)
    go_in(6, 9)
    go_out(0, 3)
    data_terms(1)
    relay_grad_cols(forwards, range(1, nc))
    p_sent = merge_terms(1)
    go_in(9, 12)
    go_out(3, 7)
    for _, passed, _ in forwards:
        passed[0].wait_recv()
    group_terms(0, True, nc == 1)
    go_in(12, 18)
    go_out(7, 12)
    for t in range(1, nc):
        for _, passed, _ in forwards:
            passed[nc - t].wait_recv()
        group_terms(t, False, t == nc - 1)
        if t == 1:
            out_in[...] = part_sum(1, p_sent).astype(BF16).reshape(p, H, X, C)
    go_out(12, 18)
    for c in pending:
        c.wait_send()
    drain()


def solution(mesh):
    n, m = mesh.shape["rot"], mesh.shape["az"]

    def shards(inputs, pre_one, pre_two, cot, filt_one, filt_two):
        p, H, X, C = inputs.shape
        R, HX, K, nc = n * p, H * X, 9 * p, n // 2
        scale = float(R * H * X * m) ** -0.5
        dma = pltpu.SemaphoreType.DMA
        vmem = pl.BlockSpec(memory_space=pltpu.VMEM)
        AZ = X * m
        sums = jax.ShapeDtypeStruct((p, 3, 3, C, C), F32)
        return pl.pallas_call(
            functools.partial(kernel, n, m, p, H, X, C, scale),
            out_shape=(jax.ShapeDtypeStruct((p, H, X, C), BF16), sums, sums),
            in_specs=[vmem] * 4 + [pl.BlockSpec(memory_space=pl.ANY)] * 2,
            out_specs=(vmem,) * 3,
            scratch_shapes=[
                pltpu.VMEM((2, p, H, X, C), BF16),
                pltpu.VMEM((2, 2, p * H, C), BF16),
                pltpu.VMEM((p, C, HX), BF16),
                pltpu.VMEM((n, p, H, X, C), BF16),
                pltpu.VMEM((2, n, 2, p * H, C), BF16),
                pltpu.VMEM((n, p, C, HX), BF16),
                pltpu.VMEM((2, p * C, 9 * C), BF16),
                pltpu.VMEM((R, H + 2, X, 3 * C), BF16),
                pltpu.VMEM((3 * C, (R + p - 1) * HX), BF16),
                pltpu.VMEM((R, HX, p * C), F32),
                pltpu.VMEM((2, n, p, HX, C), BF16),
                pltpu.VMEM((2, nc, p, HX, C), BF16),
                pltpu.VMEM((2, nc, p, HX, C), BF16),
                pltpu.VMEM((2, nc, p, HX, C), BF16),
                pltpu.VMEM((K, C, C), BF16),
                pltpu.VMEM((2, K, C, C), BF16),
                pltpu.VMEM((K, C, C), BF16),
                pltpu.VMEM((K, C, C), BF16),
                pltpu.VMEM((p, H, AZ, C), BF16),
                pltpu.VMEM((C, p * H * AZ), BF16),
                pltpu.VMEM((3 * C, R * H * AZ), BF16),
                pltpu.VMEM((R, H, AZ, C), BF16),
                pltpu.VMEM((3, 3 * C, p * C), F32),
                pltpu.VMEM((p, H, X, C), F32),
            ]
            + [dma((2, nc))] * 4
            + [dma((2, 2, nc))] * 2
            + [dma((2, nc))] * 2
            + [dma((2, nc))] * 8
            + [dma((K,)), dma((2, K)), dma((K,)), dma((K,))]
            + [dma((2, K))]
            + [dma((m,))] * 4
            + [dma((m, nc))] * 4,
            compiler_params=pltpu.CompilerParams(
                collective_id=0, has_side_effects=True, vmem_limit_bytes=60 * 1024 * 1024
            ),
        )(inputs, pre_one, pre_two, cot, filt_one, filt_two)

    cells = P("rot", None, "az", None)
    banks = P("rot", None, None, None, None)
    return jax.shard_map(
        shards, mesh=mesh,
        in_specs=(cells,) * 4 + (banks,) * 2,
        out_specs=(cells, banks, banks),
        check_vma=False,
    )
```

```python
import functools
import math

import jax
import jax.numpy as jnp
from jax import lax
from jax.experimental import pallas as pl
from jax.experimental.pallas import tpu as pltpu
from jax.sharding import PartitionSpec as P

F32 = jnp.float32
BF16 = jnp.bfloat16


def slope(v):
    s = jax.nn.sigmoid(v)
    return s * (1.0 + v * (1.0 - s))


def kernel(
    n, m, p, H, X, C, scale,
    inputs_at, pre_one_at, pre_two_at, cot_at, filt_one, filt_two,
    out_in, out_f1, out_f2,
    inputs, pre_one, pre_two, cot, made_one, made_two,
    st_g, st_e, st_a, grads, edges, feats, weights, gx, lhs, outs,
    part_s, part_x, part_m, part_r, zs, zr, zt, zf,
    field_in, whole_in, whole_g, acc, turn,
    g_ss, g_rs, gf_ss, gf_rs, e_ss, e_rs, ef_ss, ef_rs, a_ss, a_rs, af_ss, af_rs,
    x_ss, x_rs, p_ss, p_rs, z_ss, z_rs, y_ss, y_rs,
    w_sem, v_sem, o_sem, cz_ss, cz_rs, h_ss, h_rs, hf_ss, hf_rs,
):
    R = n * p
    HX = H * X
    nc = n // 2
    K = 9 * p
    AZ = m * X
    me = lax.axis_index("rot")
    z = lax.axis_index("az")
    core = lax.rem(me, 2)
    chip = lax.div(me, 2)
    sib = me + 1 - 2 * core

    def to(t):
        return 2 * lax.rem(chip + t, nc) + core

    def frm(t):
        return 2 * lax.rem(chip + nc - t, nc) + core

    def col(d):
        return lax.rem(z + d, m)

    def col_at(zz):
        return pl.ds(pl.multiple_of(zz * X, X), X)

    def g_at(owner, target_chip):
        return pl.ds(p * lax.rem(owner - 2 * target_chip + n, n), p)

    def a_at(owner, target):
        slot = lax.rem(owner - 2 * lax.div(target, 2) - target + 2 * n, n)
        return pl.ds(p * slot, p)

    def copy(src, dst, ss, rs, rot, az):
        return pltpu.make_async_remote_copy(
            src_ref=src, dst_ref=dst, send_sem=ss, recv_sem=rs,
            device_id={"rot": rot, "az": az}, device_id_type=pl.DeviceIdType.MESH,
        )

    lower = z < m // 2
    near_pos = jnp.where(lower, z, m - 1 - z)
    nearest = [sorted((c for c in range(m) if c != v), key=lambda c: (abs(c - v), c)) for v in range(m // 2)]

    def other(k):
        c = nearest[0][k]
        for v in range(1, m // 2):
            c = jnp.where(near_pos == v, nearest[v][k], c)
        return jnp.where(lower, c, m - 1 - c)

    loads = [
        [
            pltpu.make_async_copy(
                filt.at[s, i, j],
                weights.at[l, pl.ds(s * C, C), pl.ds((i * 3 + j) * C, C)],
                w_sem.at[l, (s * 3 + i) * 3 + j],
            )
            for s in range(p) for i in range(3) for j in range(3)
        ]
        for l, filt in enumerate((filt_two, filt_one))
    ]
    fetch = [
        pltpu.make_async_copy(a, b, v_sem.at[k])
        for k, (a, b) in enumerate(
            ((cot_at, cot), (pre_two_at, pre_two), (pre_one_at, pre_one), (inputs_at, inputs),
             (inputs_at, field_in.at[a_at(me, me), :, col_at(z), :]))
        )
    ]
    for load in fetch + loads[0] + loads[1]:
        load.start()

    barrier = pltpu.get_barrier_semaphore()
    near_cols = sorted({1 % m, (m - 1) % m})
    partners = [(sib, z)] + [(to(t), z) for t in range(1, nc)]
    partners += [(to(t), col(d)) for d in near_cols for t in range(nc)]
    partners += [(me, col(d)) for d in range(1, m) if d not in near_cols]
    for rot, az in partners:
        pl.semaphore_signal(
            barrier, inc=1, device_id={"rot": rot, "az": az},
            device_id_type=pl.DeviceIdType.MESH,
        )

    pending = []
    leaving = []

    def leave(made, out, f, k):
        c = pltpu.make_async_copy(made.at[k], out.at[k], o_sem.at[f, k])
        c.start()
        leaving.append(c)

    def start(c):
        c.start()
        pending.append(c)
        return c

    def stage_grad(ph, value):
        st_g[ph] = value.astype(BF16)
        if ph == 0:
            grads[me] = value.astype(BF16)
        else:
            whole_g[g_at(me, chip), :, col_at(z), :] = value.astype(BF16)
        st_e[ph, 0] = value[:, :, 0, :].reshape(p * H, C).astype(BF16)
        st_e[ph, 1] = value[:, :, X - 1, :].reshape(p * H, C).astype(BF16)

    def home(ph, owner, target_chip, zz):
        if ph == 0:
            return grads.at[owner]
        return whole_g.at[g_at(owner, target_chip), :, col_at(zz), :]

    def there(t):
        return lax.rem(chip + t, nc)

    def send_grad(ph):
        rims = []
        for t in range(nc):
            for side, d in ((1, 1), (0, m - 1)):
                rims.append(
                    start(
                        copy(
                            st_e.at[ph, side], edges.at[ph, me, 1 - side],
                            e_ss.at[ph, side, t], e_rs.at[ph, side, t], to(t), col(d),
                        )
                    )
                )
        direct = [None] + [
            start(copy(st_g.at[ph], home(ph, me, there(t), z), g_ss.at[ph, t], g_rs.at[ph, t], to(t), z))
            for t in range(1, nc)
        ]
        own = start(copy(st_g.at[ph], home(ph, me, chip, z), gf_ss.at[ph, 0], gf_rs.at[ph, 0], sib, z))
        return direct, own, rims

    def relay_grad(ph, sent):
        direct, own, rims = sent
        passed = [own]
        for t in range(nc):
            rims[2 * t].wait_recv()
            rims[2 * t + 1].wait_recv()
            d = frm(t)
            passed.append(
                start(copy(edges.at[ph, d], edges.at[ph, d], ef_ss.at[ph, t], ef_rs.at[ph, t], sib, z))
            )
        for t in range(1, nc):
            direct[t].wait_recv()
            d = frm(t)
            passed.append(
                start(copy(home(ph, d, chip, z), home(ph, d, chip, z), gf_ss.at[ph, t], gf_rs.at[ph, t], sib, z))
            )
        return passed

    def stage_feat(value):
        for o in range(p):
            turned = value[o].T.astype(BF16)
            st_a[o] = turned
            feats[me, o] = turned

    def send_feat():
        direct = [None] + [
            start(copy(st_a, feats.at[me], a_ss.at[0, t], a_rs.at[0, t], to(t), z))
            for t in range(1, nc)
        ]
        own = start(copy(st_a, feats.at[me], af_ss.at[0, 0], af_rs.at[0, 0], sib, z))
        return direct, own

    def relay_feat(sent):
        direct, own = sent
        passed = [own]
        for t in range(1, nc):
            direct[t].wait_recv()
            d = frm(t)
            passed.append(
                start(copy(feats.at[d], feats.at[d], af_ss.at[0, t], af_rs.at[0, t], sib, z))
            )
        return passed

    def source(f):
        return st_g.at[1] if f else inputs

    def place(f, owner, target, zz):
        if f:
            return whole_g.at[g_at(owner, lax.div(target, 2)), :, col_at(zz), :]
        return field_in.at[a_at(owner, target), :, col_at(zz), :]

    def send_cols(f):
        return [
            start(copy(source(f), place(f, me, me, z), cz_ss.at[f, k], cz_rs.at[f, z], me, other(k)))
            for k in range(m - 1)
        ]

    def spread_at(f, k, zz, src):
        passed = [start(copy(src, place(f, me, sib, zz), hf_ss.at[f, k, 0], hf_rs.at[f, k, 0], sib, z))]
        direct = [None] + [
            start(copy(src, place(f, me, to(t), zz), h_ss.at[f, k, t], h_rs.at[f, k, t], to(t), z))
            for t in range(1, nc)
        ]
        return zz, passed, direct

    def spread_col(f, k):
        zz = other(k)
        here = place(f, me, me, zz)
        copy(here, here, cz_ss.at[f, k], cz_rs.at[f, zz], me, zz).wait_recv()
        return spread_at(f, k, zz, here)

    def relay_cols(f, k, forward):
        zz, passed, direct = forward
        for t in range(1, nc):
            direct[t].wait_recv()
            d = frm(t)
            passed.append(
                start(
                    copy(place(f, d, me, zz), place(f, d, sib, zz), hf_ss.at[f, k, t], hf_rs.at[f, k, t], sib, z)
                )
            )

    def turn_group(t):
        def body(v, carry):
            for y in range(H):
                at = pl.ds(pl.multiple_of((v * H + y) * AZ, AZ), AZ)
                a = field_in[v, y].T
                whole_in[C : 2 * C, at] = a
                whole_in[0:C, at] = pltpu.roll(a, 1, 1)
                whole_in[2 * C : 3 * C, at] = pltpu.roll(a, AZ - 1, 1)
            return carry

        lax.fori_loop(2 * p * t, 2 * p * (t + 1), body, 0)

    def group_terms(t, first, last):
        vs = list(range(2 * p * t, 2 * p * (t + 1)))
        if t == 0:
            vs = vs[p - 1 :]
        if last:
            vs = vs + list(range(p - 1))
        for i in range(3):
            low, high = max(0, i - 1), min(H, H + i - 1)
            left = jnp.concatenate(
                [whole_in[:, (v * H + low) * AZ : (v * H + high) * AZ] for v in vs], axis=1
            )
            count = (high - low) * AZ
            right = jnp.concatenate(
                [
                    jnp.concatenate(
                        [
                            whole_g[(v - s) % R, low + 1 - i : high + 1 - i].reshape(count, C)
                            for v in vs
                        ],
                        axis=0,
                    )
                    for s in range(p)
                ],
                axis=1,
            )
            got = jnp.dot(left, right, preferred_element_type=F32)
            if not first:
                got = got + acc[i]
            if not last:
                acc[i] = got
            else:
                for s in range(p):
                    for j in range(3):
                        k = (s * 3 + i) * 3 + j
                        made_one[k] = got[j * C : (j + 1) * C, s * C : (s + 1) * C] * scale
                        leave(made_one, out_f1, 0, k)

    def arrive(copies):
        for c in copies:
            c.wait_recv()

    def build_gx(ph):
        x_of = lax.broadcasted_iota(jnp.int32, (p * H, X, C), 1).reshape(p * HX, C)

        def body(d, carry):
            g = grads[d] if ph == 0 else whole_g[g_at(d, chip), :, col_at(z), :]
            g = g.astype(F32).reshape(p * HX, C)
            low = edges[ph, d, 0].astype(F32)
            high = edges[ph, d, 1].astype(F32)
            low = jnp.broadcast_to(low[:, None, :], (p * H, X, C)).reshape(p * HX, C)
            high = jnp.broadcast_to(high[:, None, :], (p * H, X, C)).reshape(p * HX, C)
            before = jnp.where(x_of == 0, low, pltpu.roll(g, 1, 0))
            after = jnp.where(x_of == X - 1, high, pltpu.roll(g, p * HX - 1, 0))
            for j, v in enumerate((after, g, before)):
                gx[pl.ds(d * p, p), 1 : H + 1, :, j * C : (j + 1) * C] = v.astype(BF16).reshape(p, H, X, C)
            return carry

        lax.fori_loop(0, n, body, 0)

    def build_lhs():
        lane = lax.broadcasted_iota(jnp.int32, (C, HX), 1)
        for q in range(n):
            owner = lax.rem(me + q, n)
            for o in range(p):
                block = q * p + o
                a = feats[owner, o]
                wide = a.astype(F32)
                down = jnp.where(lane < X, 0.0, pltpu.roll(wide, X, 1)).astype(BF16)
                up = jnp.where(lane >= HX - X, 0.0, pltpu.roll(wide, HX - X, 1)).astype(BF16)
                spots = [block] + ([R + block] if block < p - 1 else [])
                for spot in spots:
                    for i, v in enumerate((down, a, up)):
                        lhs[i * C : (i + 1) * C, spot * HX : (spot + 1) * HX] = v

    def term(q, o):
        total = None
        for s in range(p):
            one = outs[(q * p + o - s) % R, :, s * C : (s + 1) * C]
            total = one if total is None else total + one
        return total

    def data_terms(ph, beside):
        for load in loads[ph]:
            load.wait()
        w = weights[ph]
        crossed = [None] * n

        def emit(q):
            for o in range(p):
                part_s[ph, q, o] = term(q, o).astype(BF16)
            t = lax.rem(q // 2 + core, nc)
            crossed[q] = start(
                copy(part_s.at[ph, q], part_x.at[ph, t], x_ss.at[ph, t], x_rs.at[ph, t], sib, z)
            )

        for q in range(n):
            rows = jnp.concatenate(
                [gx[q * p : (q + 1) * p, 2 - i : 2 - i + H].reshape(p * HX, 3 * C) for i in range(3)],
                axis=1,
            )
            got = lax.dot_general(rows, w, (((1,), (1,)), ((), ())), preferred_element_type=F32)
            outs[q * p : (q + 1) * p] = got.reshape(p, HX, p * C)
            if q % 2 == 1:
                emit(q)
            if q in beside:
                beside[q]()

    def merge_terms(ph):
        sent = []
        for t in list(range(1, nc)) + [0]:
            pltpu.make_async_remote_copy(
                src_ref=part_x.at[ph, t], dst_ref=part_x.at[ph, t],
                send_sem=x_ss.at[ph, t], recv_sem=x_rs.at[ph, t],
                device_id={"rot": sib, "az": z}, device_id_type=pl.DeviceIdType.MESH,
            ).wait_recv()
            for o in range(p):
                total = term(2 * t, o) + part_x[ph, t, o].astype(F32)
                if t == 0:
                    part_r[ph, 0, o] = total.astype(BF16)
                else:
                    part_m[ph, t, o] = total.astype(BF16)
            if t > 0:
                sent.append(
                    start(
                        copy(part_m.at[ph, t], part_r.at[ph, t], p_ss.at[ph, t], p_rs.at[ph, t], to(t), z)
                    )
                )
        return sent

    def part_sum(ph, copies):
        arrive(copies)
        total = part_r[ph, 0].astype(F32)
        for t in range(1, nc):
            total = total + part_r[ph, t].astype(F32)
        return total

    right, left = jnp.minimum(z + 1, m - 1), jnp.maximum(z - 1, 0)
    inner = jnp.where(lower, right, left)
    outer = jnp.where(lower, left, right)
    at_end = near_pos == 0
    at_mid = near_pos == m // 2 - 1
    slot = jnp.where(at_mid, 1, 0)

    def inward(src, k):
        return copy(src, zr.at[slot, k], z_ss.at[k], z_rs.at[slot, k], me, inner)

    def crossed_in(w, k):
        return copy(zr.at[w, k], zr.at[w, k], z_ss.at[k], z_rs.at[w, k], me, inner)

    def outward(k):
        return copy(zf.at[k], zf.at[k], y_ss.at[k], y_rs.at[k], me, outer)

    def filt_terms():
        right_side = gx[:, 1 : H + 1].reshape(R * HX, 3 * C)
        for s in range(p):
            got = jnp.dot(
                lhs[:, s * HX : (s + R) * HX], right_side, preferred_element_type=F32
            )
            for i in range(3):
                for j in range(3):
                    zs[(s * 3 + i) * 3 + j] = got[i * C : (i + 1) * C, j * C : (j + 1) * C].astype(BF16)
            if s == 0:
                begin(0, min(7, 18 // p))

    def begin(a, b):
        @pl.when(at_end)
        def _():
            for k in range(K * a // 18, K * b // 18):
                inward(zs.at[k], k).start()

    def go_in(a, b):
        @pl.when(jnp.logical_not(at_end))
        def _():
            for k in range(K * a // 18, K * b // 18):
                crossed_in(0, k).wait_recv()
                zt[k] = (zs[k].astype(F32) + zr[0, k].astype(F32)).astype(BF16)
                inward(zt.at[k], k).start()

    base = zs if m == 2 else zt

    def cross(a, b):
        @pl.when(at_mid)
        def _():
            for k in range(K * a // 18, K * b // 18):
                crossed_in(1, k).wait_recv()
                zf[k] = (base[k].astype(F32) + zr[1, k].astype(F32)).astype(BF16)

                @pl.when(jnp.logical_not(at_end))
                def _():
                    outward(k).start()

    def settle(a, b):
        for k in range(K * a // 18, K * b // 18):

            @pl.when(jnp.logical_not(at_mid))
            def _():
                outward(k).wait_recv()

                @pl.when(jnp.logical_not(at_end))
                def _():
                    outward(k).start()

            made_two[k] = zf[k].astype(F32) * scale
            leave(made_two, out_f2, 1, k)

    def drain():
        for k in range(K):
            crossed_in(0, k).wait_send()

        @pl.when(jnp.logical_not(at_end))
        def _():
            for k in range(K):
                outward(k).wait_send()

    fetch[0].wait()
    fetch[1].wait()
    grad_two = (cot[...].astype(F32) * slope(pre_two[...].astype(F32))).astype(BF16).astype(F32)
    stage_grad(0, grad_two)
    fetch[2].wait()
    wide_one = pre_one[...].astype(F32)
    stage_feat((wide_one * jax.nn.sigmoid(wide_one)).reshape(p, HX, C))
    turn[...] = slope(wide_one)
    gx[:, 0] = jnp.zeros((R, X, 3 * C), BF16)
    gx[:, H + 1] = jnp.zeros((R, X, 3 * C), BF16)
    fetch[3].wait()
    fetch[4].wait()
    pl.semaphore_wait(barrier, len(partners))
    g_sent = send_grad(0)
    send_cols(0)
    a_sent = send_feat()
    moves = {(0, m - 1): spread_at(0, m - 1, z, inputs)}

    def spread(f, *ks):
        for k in ks:
            if k < m - 1:
                moves[f, k] = spread_col(f, k)

    def relay(f, *ks):
        for k in ks:
            relay_cols(f, k, moves[f, k])

    kept = {}
    g_passed = relay_grad(0, g_sent)
    spread(0, 0)
    arrive(g_passed)
    build_gx(0)
    data_terms(0, {
        n // 8: lambda: spread(0, 1),
        n // 2: lambda: kept.update(a=relay_feat(a_sent)),
    })
    arrive(kept["a"])
    build_lhs()
    p_sent = merge_terms(0)
    spread(0, *range(2, m - 1))
    filt_terms()
    relay(0, m - 1, *range(min(2, m - 1)))

    delta = part_sum(0, p_sent).reshape(p, H, X, C)
    grad_one = (delta * turn[...]).astype(BF16).astype(F32)
    stage_grad(1, grad_one)
    g_sent = send_grad(1)
    send_cols(1)
    begin(min(7, 18 // p), 18)
    relay(0, *range(2, m - 1))
    go_in(0, 7)
    for k in range(m):
        arrive(moves[0, k][1])
    half = nc // 2
    for t in range(half):
        turn_group(t)
    spread(1, 0)
    g_passed = relay_grad(1, g_sent)
    arrive(g_passed)
    build_gx(1)
    data_terms(1, {
        n // 4: lambda: spread(1, 1),
        3 * n // 4: lambda: spread(1, *range(2, m - 1)),
    })
    go_in(7, 11)
    p_sent = merge_terms(1)
    for t in range(half, nc):
        turn_group(t)
    relay(1, *range(min(2, m - 1)))
    go_in(11, 18)
    cross(0, 7)
    relay(1, *range(2, m - 1))
    cols = [moves[1, k][1] for k in range(m - 1)]
    for passed in cols:
        passed[0].wait_recv()
    group_terms(0, True, nc == 1)
    settle(0, 7)
    cross(7, 11)
    out_in[...] = part_sum(1, p_sent).astype(BF16).reshape(p, H, X, C)
    for t in range(1, nc):
        for passed in cols:
            passed[nc - t].wait_recv()
        group_terms(t, False, t == nc - 1)
        if t == 1:
            settle(7, 11)
            cross(11, 18)
    settle(11, 18)
    for c in pending:
        c.wait_send()
    drain()
    for c in leaving:
        c.wait()


def emit(got, sum_one, sum_two, out, out_one, out_two, sems):
    moves = [
        pltpu.make_async_copy(a, b, sems.at[k])
        for k, (a, b) in enumerate(((sum_one, out_one), (sum_two, out_two), (got, out)))
    ]
    for c in moves:
        c.start()
    for c in moves:
        c.wait()


def solution(mesh):
    n, m = mesh.shape["rot"], mesh.shape["az"]

    def shards(inputs, pre_one, pre_two, cot, filt_one, filt_two):
        p, H, X, C = inputs.shape
        R, HX, K, nc = n * p, H * X, 9 * p, n // 2
        scale = float(R * H * X * m) ** -0.5
        dma = pltpu.SemaphoreType.DMA
        vmem = pl.BlockSpec(memory_space=pltpu.VMEM)
        AZ = X * m
        anywhere = pl.BlockSpec(memory_space=pl.ANY)
        sums = jax.ShapeDtypeStruct((K, C, C), F32)
        scratch = [
            pltpu.VMEM((p, H, X, C), BF16),
            pltpu.VMEM((p, H, X, C), BF16),
            pltpu.VMEM((p, H, X, C), BF16),
            pltpu.VMEM((p, H, X, C), BF16),
            pltpu.VMEM((K, C, C), F32),
            pltpu.VMEM((K, C, C), F32),
        pltpu.VMEM((2, p, H, X, C), BF16),
        pltpu.VMEM((2, 2, p * H, C), BF16),
        pltpu.VMEM((p, C, HX), BF16),
        pltpu.VMEM((n, p, H, X, C), BF16),
        pltpu.VMEM((2, n, 2, p * H, C), BF16),
        pltpu.VMEM((n, p, C, HX), BF16),
        pltpu.VMEM((2, p * C, 9 * C), BF16),
        pltpu.VMEM((R, H + 2, X, 3 * C), BF16),
        pltpu.VMEM((3 * C, (R + p - 1) * HX), BF16),
        pltpu.VMEM((R, HX, p * C), F32),
        pltpu.VMEM((2, n, p, HX, C), BF16),
        pltpu.VMEM((2, nc, p, HX, C), BF16),
        pltpu.VMEM((2, nc, p, HX, C), BF16),
        pltpu.VMEM((2, nc, p, HX, C), BF16),
        pltpu.VMEM((K, C, C), BF16),
        pltpu.VMEM((2, K, C, C), BF16),
        pltpu.VMEM((K, C, C), BF16),
        pltpu.VMEM((K, C, C), BF16),
        pltpu.VMEM((R, H, AZ, C), BF16),
        pltpu.VMEM((3 * C, R * H * AZ), BF16),
        pltpu.VMEM((R, H, AZ, C), BF16),
        pltpu.VMEM((3, 3 * C, p * C), F32),
        pltpu.VMEM((p, H, X, C), F32),
        ]
        held = sum(math.prod(v.shape) * jnp.dtype(v.dtype).itemsize for v in scratch)
        held += 2 * inputs.size
        made = pl.pallas_call(
            functools.partial(kernel, n, m, p, H, X, C, scale),
            out_shape=(jax.ShapeDtypeStruct((p, H, X, C), BF16), sums, sums),
            in_specs=[pl.BlockSpec(memory_space=pltpu.HBM)] * 6,
            out_specs=(vmem, anywhere, anywhere),
            scratch_shapes=scratch
            + [dma((2, nc))] * 4
            + [dma((2, 2, nc))] * 2
            + [dma((2, nc))] * 2
            + [dma((2, nc))] * 8
            + [dma((K,)), dma((2, K)), dma((K,)), dma((K,))]
            + [dma((2, K)), dma((5,)), dma((2, K))]
            + [dma((2, m))] * 2
            + [dma((2, m, nc))] * 4,
            compiler_params=pltpu.CompilerParams(
                collective_id=0, has_side_effects=True, vmem_limit_bytes=held + 3 * 1024 * 1024
            ),
        )(*(pltpu.with_memory_space_constraint(v, pltpu.HBM) for v in (inputs, pre_one, pre_two, cot, filt_one, filt_two)))
        got, one, two = pl.pallas_call(
            emit,
            out_shape=tuple(jax.ShapeDtypeStruct(v.shape, v.dtype) for v in made),
            in_specs=[vmem] * 3,
            out_specs=(anywhere,) * 3,
            scratch_shapes=[dma((3,))],
            compiler_params=pltpu.CompilerParams(vmem_limit_bytes=4 * 1024 * 1024),
        )(*made)
        return got, one.reshape(p, 3, 3, C, C), two.reshape(p, 3, 3, C, C)

    cells = P("rot", None, "az", None)
    banks = P("rot", None, None, None, None)
    return jax.shard_map(
        shards, mesh=mesh,
        in_specs=(cells,) * 4 + (banks,) * 2,
        out_specs=(cells, banks, banks),
        check_vma=False,
    )
```

```python
import functools
import math

import jax
import jax.numpy as jnp
from jax import lax
from jax.experimental import pallas as pl
from jax.experimental.pallas import tpu as pltpu
from jax.sharding import PartitionSpec as P

F32 = jnp.float32
BF16 = jnp.bfloat16


def slope(v):
    s = jax.nn.sigmoid(v)
    return s * (1.0 + v * (1.0 - s))


def kernel(
    n, m, p, H, X, C,
    inputs_at, pre_one_at, pre_two_at, cot_at, filt_one, filt_two,
    out_in, out_f1, out_f2,
    inputs, pre_one, pre_two, cot,
    st_g, st_e, st_a, grads, edges, feats, weights, gx, lhs, outs,
    part_s, part_x, part_m, part_r, zs, zr, zt,
    field_in, whole_in, whole_g, acc, turn,
    g_ss, g_rs, gf_ss, gf_rs, e_ss, e_rs, ef_ss, ef_rs, a_ss, a_rs, af_ss, af_rs,
    x_ss, x_rs, p_ss, p_rs, z_ss, z_rs, y_ss, y_rs,
    w_sem, v_sem, cz_ss, cz_rs, h_ss, h_rs, hf_ss, hf_rs,
):
    R = n * p
    HX = H * X
    nc = n // 2
    K = 9 * p
    me = lax.axis_index("rot")
    z = lax.axis_index("az")
    core = lax.rem(me, 2)
    chip = lax.div(me, 2)
    sib = me + 1 - 2 * core

    def to(t):
        return 2 * lax.rem(chip + t, nc) + core

    def frm(t):
        return 2 * lax.rem(chip + nc - t, nc) + core

    def col(d):
        return lax.rem(z + d, m)

    def g_at(owner, target_chip):
        return pl.ds(p * lax.rem(owner - 2 * target_chip + n, n), p)

    def a_at(owner, target):
        slot = lax.rem(owner - 2 * lax.div(target, 2) - target + 2 * n, n)
        return pl.ds(p * slot, p)

    def copy(src, dst, ss, rs, rot, az):
        return pltpu.make_async_remote_copy(
            src_ref=src, dst_ref=dst, send_sem=ss, recv_sem=rs,
            device_id={"rot": rot, "az": az}, device_id_type=pl.DeviceIdType.MESH,
        )

    lower = z < m // 2
    near_pos = jnp.where(lower, z, m - 1 - z)
    nearest = [sorted((c for c in range(m) if c != v), key=lambda c: (abs(c - v), c)) for v in range(m // 2)]

    def other(k):
        c = nearest[0][k]
        for v in range(1, m // 2):
            c = jnp.where(near_pos == v, nearest[v][k], c)
        return jnp.where(lower, c, m - 1 - c)

    loads = [
        [
            pltpu.make_async_copy(
                filt.at[s, i, j],
                weights.at[l, pl.ds(s * C, C), pl.ds((i * 3 + j) * C, C)],
                w_sem.at[l, (s * 3 + i) * 3 + j],
            )
            for s in range(p) for i in range(3) for j in range(3)
        ]
        for l, filt in enumerate((filt_two, filt_one))
    ]
    fetch = [
        pltpu.make_async_copy(a, b, v_sem.at[k])
        for k, (a, b) in enumerate(
            ((cot_at, cot), (pre_two_at, pre_two), (pre_one_at, pre_one), (inputs_at, inputs),
             (inputs_at, field_in.at[a_at(me, me), z]))
        )
    ]
    for load in fetch + loads[0] + loads[1]:
        load.start()

    barrier = pltpu.get_barrier_semaphore()
    near_cols = sorted({1 % m, (m - 1) % m})
    partners = [(sib, z)] + [(to(t), z) for t in range(1, nc)]
    partners += [(to(t), col(d)) for d in near_cols for t in range(nc)]
    partners += [(me, col(d)) for d in range(1, m) if d not in near_cols]
    for rot, az in partners:
        pl.semaphore_signal(
            barrier, inc=1, device_id={"rot": rot, "az": az},
            device_id_type=pl.DeviceIdType.MESH,
        )

    pending = []
    def start(c):
        c.start()
        pending.append(c)
        return c

    def stage_grad(ph, value):
        st_g[ph] = value.astype(BF16)
        if ph == 0:
            grads[me] = value.astype(BF16)
        else:
            whole_g[g_at(me, chip), z, 1 : H + 1] = value.astype(BF16)
        st_e[ph, 0] = value[:, :, 0, :].reshape(p * H, C).astype(BF16)
        st_e[ph, 1] = value[:, :, X - 1, :].reshape(p * H, C).astype(BF16)

    def home(ph, owner, target_chip, zz):
        if ph == 0:
            return grads.at[owner]
        return whole_g.at[g_at(owner, target_chip), zz, pl.ds(1, H)]

    def there(t):
        return lax.rem(chip + t, nc)

    def send_grad(ph):
        rims = []
        for t in range(nc):
            for side, d in ((1, 1), (0, m - 1)):
                rims.append(
                    start(
                        copy(
                            st_e.at[ph, side], edges.at[ph, me, 1 - side],
                            e_ss.at[ph, side, t], e_rs.at[ph, side, t], to(t), col(d),
                        )
                    )
                )
        direct = [None] + [
            start(copy(st_g.at[ph], home(ph, me, there(t), z), g_ss.at[ph, t], g_rs.at[ph, t], to(t), z))
            for t in range(1, nc)
        ]
        own = start(copy(st_g.at[ph], home(ph, me, chip, z), gf_ss.at[ph, 0], gf_rs.at[ph, 0], sib, z))
        return direct, own, rims

    def relay_grad(ph, sent):
        direct, own, rims = sent
        passed = [own]
        for t in range(nc):
            rims[2 * t].wait_recv()
            rims[2 * t + 1].wait_recv()
            d = frm(t)
            passed.append(
                start(copy(edges.at[ph, d], edges.at[ph, d], ef_ss.at[ph, t], ef_rs.at[ph, t], sib, z))
            )
        for t in range(1, nc):
            direct[t].wait_recv()
            d = frm(t)
            passed.append(
                start(copy(home(ph, d, chip, z), home(ph, d, chip, z), gf_ss.at[ph, t], gf_rs.at[ph, t], sib, z))
            )
        return passed

    def stage_feat(value):
        for o in range(p):
            turned = value[o].T.astype(BF16)
            st_a[o] = turned
            feats[me, o] = turned

    def send_feat():
        direct = [None] + [
            start(copy(st_a, feats.at[me], a_ss.at[0, t], a_rs.at[0, t], to(t), z))
            for t in range(1, nc)
        ]
        own = start(copy(st_a, feats.at[me], af_ss.at[0, 0], af_rs.at[0, 0], sib, z))
        return direct, own

    def relay_feat(sent):
        direct, own = sent
        passed = [own]
        for t in range(1, nc):
            direct[t].wait_recv()
            d = frm(t)
            passed.append(
                start(copy(feats.at[d], feats.at[d], af_ss.at[0, t], af_rs.at[0, t], sib, z))
            )
        return passed

    def source(f):
        return st_g.at[1] if f else inputs

    def place(f, owner, target, zz):
        if f:
            return home(1, owner, lax.div(target, 2), zz)
        return field_in.at[a_at(owner, target), zz]

    def send_cols(f):
        return [
            start(copy(source(f), place(f, me, me, z), cz_ss.at[f, k], cz_rs.at[f, z], me, other(k)))
            for k in range(m - 1)
        ]

    def spread_at(f, k, zz, src):
        passed = [start(copy(src, place(f, me, sib, zz), hf_ss.at[f, k, 0], hf_rs.at[f, k, 0], sib, z))]
        direct = [None] + [
            start(copy(src, place(f, me, to(t), zz), h_ss.at[f, k, t], h_rs.at[f, k, t], to(t), z))
            for t in range(1, nc)
        ]
        return zz, passed, direct

    def spread_col(f, k):
        zz = other(k)
        here = place(f, me, me, zz)
        copy(here, here, cz_ss.at[f, k], cz_rs.at[f, zz], me, zz).wait_recv()
        return spread_at(f, k, zz, here)

    def relay_cols(f, k, forward):
        zz, passed, direct = forward
        for t in range(1, nc):
            direct[t].wait_recv()
            d = frm(t)
            passed.append(
                start(
                    copy(place(f, d, me, zz), place(f, d, sib, zz), hf_ss.at[f, k, t], hf_rs.at[f, k, t], sib, z)
                )
            )

    def turn_col(zz):
        x_of = lax.broadcasted_iota(jnp.int32, (H, X, C), 1).reshape(HX, C)
        many = 4 if R % 4 == 0 else 1

        def rim(v, c, x):
            edge = field_in[v, c].astype(F32)[:, x, :]
            return jnp.broadcast_to(edge[:, None, :], (H, X, C)).reshape(HX, C)

        def body(b, carry):
            for u in range(many):
                v = b * many + u
                at = pl.ds(pl.multiple_of((zz * R + v) * HX, HX), HX)
                a = field_in[v, zz].reshape(HX, C)
                wide = a.astype(F32)
                low = rim(v, lax.rem(zz + m - 1, m), X - 1)
                high = rim(v, lax.rem(zz + 1, m), 0)
                before = jnp.where(x_of == 0, low, pltpu.roll(wide, 1, 0))
                after = jnp.where(x_of == X - 1, high, pltpu.roll(wide, HX - 1, 0))
                whole_in[0:C, at] = before.astype(BF16).T
                whole_in[C : 2 * C, at] = a.T
                whole_in[2 * C : 3 * C, at] = after.astype(BF16).T
            return carry

        lax.fori_loop(0, R // many, body, 0)

    def column(step):
        if m != 4:
            return step
        return z if step == 0 else other(step - 1)

    def col_terms(step):
        zz = column(step)
        for i in range(3):
            left = whole_in[:, pl.ds(pl.multiple_of(zz * R * HX, R * HX), R * HX)]
            sides = []
            for s in range(p):
                rows = [whole_g[R - s : R, zz, 2 - i : 2 - i + H].reshape(s * HX, C)] if s else []
                rows.append(whole_g[0 : R - s, zz, 2 - i : 2 - i + H].reshape((R - s) * HX, C))
                sides.append(jnp.concatenate(rows, axis=0))
            got = jnp.dot(left, jnp.concatenate(sides, axis=1), preferred_element_type=F32)
            if step == m - 1:
                if m == 4:
                    got = got + acc[1, i]
                got = got + acc[0, i]
                for s in range(p):
                    for j in range(3):
                        out_f1[(s * 3 + i) * 3 + j] = got[j * C : (j + 1) * C, s * C : (s + 1) * C].astype(BF16)
            elif step == 0 or (m == 4 and step == 2):
                acc[step // 2, i] = got
            else:
                acc[0, i] = acc[0, i] + got

    def arrive(copies):
        for c in copies:
            c.wait_recv()

    def build_gx(ph):
        x_of = lax.broadcasted_iota(jnp.int32, (p * H, X, C), 1).reshape(p * HX, C)

        def body(d, carry):
            g = grads[d] if ph == 0 else whole_g[g_at(d, chip), z, 1 : H + 1]
            g = g.astype(F32).reshape(p * HX, C)
            low = edges[ph, d, 0].astype(F32)
            high = edges[ph, d, 1].astype(F32)
            low = jnp.broadcast_to(low[:, None, :], (p * H, X, C)).reshape(p * HX, C)
            high = jnp.broadcast_to(high[:, None, :], (p * H, X, C)).reshape(p * HX, C)
            before = jnp.where(x_of == 0, low, pltpu.roll(g, 1, 0))
            after = jnp.where(x_of == X - 1, high, pltpu.roll(g, p * HX - 1, 0))
            for j, v in enumerate((after, g, before)):
                gx[pl.ds(d * p, p), 1 : H + 1, :, j * C : (j + 1) * C] = v.astype(BF16).reshape(p, H, X, C)
            return carry

        lax.fori_loop(0, n, body, 0)

    def build_lhs():
        lane = lax.broadcasted_iota(jnp.int32, (C, HX), 1)
        for q in range(n):
            owner = lax.rem(me + q, n)
            for o in range(p):
                block = q * p + o
                a = feats[owner, o]
                wide = a.astype(F32)
                down = jnp.where(lane < X, 0.0, pltpu.roll(wide, X, 1)).astype(BF16)
                up = jnp.where(lane >= HX - X, 0.0, pltpu.roll(wide, HX - X, 1)).astype(BF16)
                spots = [block] + ([R + block] if block < p - 1 else [])
                for spot in spots:
                    for i, v in enumerate((down, a, up)):
                        lhs[i * C : (i + 1) * C, spot * HX : (spot + 1) * HX] = v

    def term(q, o):
        total = None
        for s in range(p):
            one = outs[(q * p + o - s) % R, :, s * C : (s + 1) * C]
            total = one if total is None else total + one
        return total

    def data_terms(ph, beside):
        for load in loads[ph]:
            load.wait()
        w = weights[ph]
        crossed = [None] * n

        def emit(q):
            for o in range(p):
                part_s[ph, q, o] = term(q, o).astype(BF16)
            t = lax.rem(q // 2 + core, nc)
            crossed[q] = start(
                copy(part_s.at[ph, q], part_x.at[ph, t], x_ss.at[ph, t], x_rs.at[ph, t], sib, z)
            )

        for q in range(n):
            rows = jnp.concatenate(
                [gx[q * p : (q + 1) * p, 2 - i : 2 - i + H].reshape(p * HX, 3 * C) for i in range(3)],
                axis=1,
            )
            got = lax.dot_general(rows, w, (((1,), (1,)), ((), ())), preferred_element_type=F32)
            outs[q * p : (q + 1) * p] = got.reshape(p, HX, p * C)
            if q % 2 == 1:
                emit(q)
            if q in beside:
                beside[q]()

    def merge_terms(ph):
        sent = []
        for t in list(range(1, nc)) + [0]:
            pltpu.make_async_remote_copy(
                src_ref=part_x.at[ph, t], dst_ref=part_x.at[ph, t],
                send_sem=x_ss.at[ph, t], recv_sem=x_rs.at[ph, t],
                device_id={"rot": sib, "az": z}, device_id_type=pl.DeviceIdType.MESH,
            ).wait_recv()
            for o in range(p):
                total = term(2 * t, o) + part_x[ph, t, o].astype(F32)
                if t == 0:
                    part_r[ph, 0, o] = total.astype(BF16)
                else:
                    part_m[ph, t, o] = total.astype(BF16)
            if t > 0:
                sent.append(
                    start(
                        copy(part_m.at[ph, t], part_r.at[ph, t], p_ss.at[ph, t], p_rs.at[ph, t], to(t), z)
                    )
                )
        return sent

    def part_sum(ph, copies):
        arrive(copies)
        total = part_r[ph, 0].astype(F32)
        for t in range(1, nc):
            total = total + part_r[ph, t].astype(F32)
        return total

    right, left = jnp.minimum(z + 1, m - 1), jnp.maximum(z - 1, 0)
    inner = jnp.where(lower, right, left)
    outer = jnp.where(lower, left, right)
    at_end = near_pos == 0
    at_mid = near_pos == m // 2 - 1
    slot = jnp.where(at_mid, 1, 0)

    def inward(src, k):
        return copy(src, zr.at[slot, k], z_ss.at[k], z_rs.at[slot, k], me, inner)

    def crossed_in(w, k):
        return copy(zr.at[w, k], zr.at[w, k], z_ss.at[k], z_rs.at[w, k], me, inner)

    def outward(k):
        return copy(out_f2.at[k], out_f2.at[k], y_ss.at[k], y_rs.at[k], me, outer)

    def filt_terms():
        right_side = gx[:, 1 : H + 1].reshape(R * HX, 3 * C)
        for s in range(p):
            got = jnp.dot(
                lhs[:, s * HX : (s + R) * HX], right_side, preferred_element_type=F32
            )
            for i in range(3):
                for j in range(3):
                    zs[(s * 3 + i) * 3 + j] = got[i * C : (i + 1) * C, j * C : (j + 1) * C].astype(BF16)
            if s == 0:
                begin(0, min(7, 18 // p))

    def begin(a, b):
        @pl.when(at_end)
        def _():
            for k in range(K * a // 18, K * b // 18):
                inward(zs.at[k], k).start()

    def go_in(a, b):
        @pl.when(jnp.logical_not(at_end))
        def _():
            for k in range(K * a // 18, K * b // 18):
                crossed_in(0, k).wait_recv()
                zt[k] = (zs[k].astype(F32) + zr[0, k].astype(F32)).astype(BF16)
                inward(zt.at[k], k).start()

    base = zs if m == 2 else zt

    def cross(a, b):
        @pl.when(at_mid)
        def _():
            for k in range(K * a // 18, K * b // 18):
                crossed_in(1, k).wait_recv()
                out_f2[k] = (base[k].astype(F32) + zr[1, k].astype(F32)).astype(BF16)

                @pl.when(jnp.logical_not(at_end))
                def _():
                    outward(k).start()

    def settle(a, b):
        for k in range(K * a // 18, K * b // 18):

            @pl.when(jnp.logical_not(at_mid))
            def _():
                outward(k).wait_recv()

                @pl.when(jnp.logical_not(at_end))
                def _():
                    outward(k).start()


    def drain():
        for k in range(K):
            crossed_in(0, k).wait_send()

        @pl.when(jnp.logical_not(at_end))
        def _():
            for k in range(K):
                outward(k).wait_send()

    fetch[0].wait()
    fetch[1].wait()
    grad_two = (cot[...].astype(F32) * slope(pre_two[...].astype(F32))).astype(BF16).astype(F32)
    stage_grad(0, grad_two)
    fetch[2].wait()
    wide_one = pre_one[...].astype(F32)
    stage_feat((wide_one * jax.nn.sigmoid(wide_one)).reshape(p, HX, C))
    turn[...] = slope(wide_one)
    gx[:, 0] = jnp.zeros((R, X, 3 * C), BF16)
    gx[:, H + 1] = jnp.zeros((R, X, 3 * C), BF16)
    whole_g[:, :, 0] = jnp.zeros((R, m, X, C), BF16)
    whole_g[:, :, H + 1] = jnp.zeros((R, m, X, C), BF16)
    fetch[3].wait()
    fetch[4].wait()
    pl.semaphore_wait(barrier, len(partners))
    g_sent = send_grad(0)
    send_cols(0)
    a_sent = send_feat()
    moves = {(0, m - 1): spread_at(0, m - 1, z, inputs)}

    def spread(f, *ks):
        for k in ks:
            if k < m - 1:
                moves[f, k] = spread_col(f, k)

    def relay(f, *ks):
        for k in ks:
            relay_cols(f, k, moves[f, k])

    kept = {}
    g_passed = relay_grad(0, g_sent)
    spread(0, 0)
    arrive(g_passed)
    build_gx(0)
    data_terms(0, {
        n // 8: lambda: spread(0, 1),
        n // 2: lambda: kept.update(a=relay_feat(a_sent)),
    })
    arrive(kept["a"])
    build_lhs()
    p_sent = merge_terms(0)
    spread(0, *range(2, m - 1))
    filt_terms()
    relay(0, m - 1, *range(min(2, m - 1)))

    delta = part_sum(0, p_sent).reshape(p, H, X, C)
    grad_one = (delta * turn[...]).astype(BF16).astype(F32)
    stage_grad(1, grad_one)
    g_sent = send_grad(1)
    send_cols(1)
    begin(min(7, 18 // p), 18)
    relay(0, *range(2, m - 1))
    go_in(0, 7)
    for k in range(m):
        arrive(moves[0, k][1])
    if m != 4:
        for c in range(m):
            turn_col(c)
    else:
        turn_col(column(0))
        turn_col(column(1))
    spread(1, 0)
    g_passed = relay_grad(1, g_sent)
    if m == 4:
        turn_col(column(2))
    arrive(g_passed)
    build_gx(1)
    data_terms(1, {
        n // 4: lambda: spread(1, 1),
        3 * n // 4: lambda: spread(1, *range(2, m - 1)),
    })
    go_in(7, 11)
    p_sent = merge_terms(1)
    cols = [moves[1, k][1] for k in range(m - 1)]
    if m == 4:
        turn_col(column(3))
        col_terms(0)
    relay(1, 0)
    go_in(11, 18)
    cross(0, 7)
    relay(1, *range(1, m - 1))
    if m == 4:
        arrive(cols[0])
        col_terms(1)
    settle(0, 7)
    cross(7, 11)
    out_in[...] = part_sum(1, p_sent).astype(BF16).reshape(p, H, X, C)
    if m == 4:
        arrive(cols[1])
        col_terms(2)
    settle(7, 11)
    cross(11, 18)
    if m == 4:
        arrive(cols[2])
        col_terms(3)
    else:
        for passed in cols:
            arrive(passed)
        for step in range(m):
            col_terms(step)
    settle(11, 18)
    for c in pending:
        c.wait_send()
    drain()


def emit(scale, got, one, two, out, out_one, out_two, wide, sems):
    k, half = one.shape[0], one.shape[0] // 3
    moves = [pltpu.make_async_copy(got, out, sems.at[0])]
    moves[0].start()
    for f, (a, b) in enumerate(((one, out_one), (two, out_two))):
        for c in range(0, k, half):
            wide[f, c : c + half] = a[c : c + half].astype(F32) * scale
            moves.append(
                pltpu.make_async_copy(
                    wide.at[f, c : c + half], b.at[c : c + half], sems.at[1 + f * 3 + c // half]
                )
            )
            moves[-1].start()
    for c in moves:
        c.wait()


def solution(mesh):
    n, m = mesh.shape["rot"], mesh.shape["az"]

    def shards(inputs, pre_one, pre_two, cot, filt_one, filt_two):
        p, H, X, C = inputs.shape
        R, HX, K, nc = n * p, H * X, 9 * p, n // 2
        scale = float(R * H * X * m) ** -0.5
        dma = pltpu.SemaphoreType.DMA
        vmem = pl.BlockSpec(memory_space=pltpu.VMEM)
        anywhere = pl.BlockSpec(memory_space=pl.ANY)
        sums = jax.ShapeDtypeStruct((K, C, C), BF16)
        scratch = [
            pltpu.VMEM((p, H, X, C), BF16),
            pltpu.VMEM((p, H, X, C), BF16),
            pltpu.VMEM((p, H, X, C), BF16),
            pltpu.VMEM((p, H, X, C), BF16),
        pltpu.VMEM((2, p, H, X, C), BF16),
        pltpu.VMEM((2, 2, p * H, C), BF16),
        pltpu.VMEM((p, C, HX), BF16),
        pltpu.VMEM((n, p, H, X, C), BF16),
        pltpu.VMEM((2, n, 2, p * H, C), BF16),
        pltpu.VMEM((n, p, C, HX), BF16),
        pltpu.VMEM((2, p * C, 9 * C), BF16),
        pltpu.VMEM((R, H + 2, X, 3 * C), BF16),
        pltpu.VMEM((3 * C, (R + p - 1) * HX), BF16),
        pltpu.VMEM((R, HX, p * C), F32),
        pltpu.VMEM((2, n, p, HX, C), BF16),
        pltpu.VMEM((2, nc, p, HX, C), BF16),
        pltpu.VMEM((2, nc, p, HX, C), BF16),
        pltpu.VMEM((2, nc, p, HX, C), BF16),
        pltpu.VMEM((K, C, C), BF16),
        pltpu.VMEM((2, K, C, C), BF16),
        pltpu.VMEM((K, C, C), BF16),
        pltpu.VMEM((R, m, H, X, C), BF16),
        pltpu.VMEM((3 * C, m * R * HX), BF16),
        pltpu.VMEM((R, m, H + 2, X, C), BF16),
        pltpu.VMEM((2, 3, 3 * C, p * C), F32),
        pltpu.VMEM((p, H, X, C), F32),
        ]
        held = sum(math.prod(v.shape) * jnp.dtype(v.dtype).itemsize for v in scratch)
        held += 2 * inputs.size + 2 * 2 * K * C * C
        made = pl.pallas_call(
            functools.partial(kernel, n, m, p, H, X, C),
            out_shape=(jax.ShapeDtypeStruct((p, H, X, C), BF16), sums, sums),
            in_specs=[pl.BlockSpec(memory_space=pltpu.HBM)] * 6,
            out_specs=(vmem,) * 3,
            scratch_shapes=scratch
            + [dma((2, nc))] * 4
            + [dma((2, 2, nc))] * 2
            + [dma((2, nc))] * 2
            + [dma((2, nc))] * 8
            + [dma((K,)), dma((2, K)), dma((K,)), dma((K,))]
            + [dma((2, K)), dma((5,))]
            + [dma((2, m))] * 2
            + [dma((2, m, nc))] * 4,
            compiler_params=pltpu.CompilerParams(
                collective_id=0, has_side_effects=True, vmem_limit_bytes=held + 3 * 1024 * 1024
            ),
        )(*(pltpu.with_memory_space_constraint(v, pltpu.HBM) for v in (inputs, pre_one, pre_two, cot, filt_one, filt_two)))
        got, one, two = pl.pallas_call(
            functools.partial(emit, scale),
            out_shape=(
                jax.ShapeDtypeStruct((p, H, X, C), BF16),
                jax.ShapeDtypeStruct((K, C, C), F32),
                jax.ShapeDtypeStruct((K, C, C), F32),
            ),
            in_specs=[vmem] * 3,
            out_specs=(anywhere,) * 3,
            scratch_shapes=[pltpu.VMEM((2, K, C, C), F32), dma((7,))],
            compiler_params=pltpu.CompilerParams(vmem_limit_bytes=8 * 1024 * 1024),
        )(*made)
        return got, one.reshape(p, 3, 3, C, C), two.reshape(p, 3, 3, C, C)

    cells = P("rot", None, "az", None)
    banks = P("rot", None, None, None, None)
    return jax.shard_map(
        shards, mesh=mesh,
        in_specs=(cells,) * 4 + (banks,) * 2,
        out_specs=(cells, banks, banks),
        check_vma=False,
    )
```

```python
import functools
import math

import jax
import jax.numpy as jnp
from jax import lax
from jax.experimental import pallas as pl
from jax.experimental.pallas import tpu as pltpu
from jax.sharding import PartitionSpec as P

F32 = jnp.float32
BF16 = jnp.bfloat16


def slope(v):
    s = jax.nn.sigmoid(v)
    return s * (1.0 + v * (1.0 - s))


def kernel(
    n, m, p, H, X, C,
    inputs_at, pre_one_at, pre_two_at, cot_at, filt_one, filt_two,
    out_in, out_f1, out_f2,
    inputs, pre_one, pre_two, cot,
    st_g, st_e, st_a, grads, edges, feats, weights, gx, lhs, outs,
    part_s, part_x, part_m, part_r, zs, zr, zt,
    field_in, whole_in, whole_g, acc, turn,
    g_ss, g_rs, gf_ss, gf_rs, e_ss, e_rs, ef_ss, ef_rs, a_ss, a_rs, af_ss, af_rs,
    x_ss, x_rs, p_ss, p_rs, z_ss, z_rs, y_ss, y_rs,
    w_sem, v_sem, cz_ss, cz_rs, h_ss, h_rs, hf_ss, hf_rs,
):
    R = n * p
    HX = H * X
    nc = n // 2
    K = 9 * p
    me = lax.axis_index("rot")
    z = lax.axis_index("az")
    core = lax.rem(me, 2)
    chip = lax.div(me, 2)
    sib = me + 1 - 2 * core

    def to(t):
        return 2 * lax.rem(chip + t, nc) + core

    def frm(t):
        return 2 * lax.rem(chip + nc - t, nc) + core

    def col(d):
        return lax.rem(z + d, m)

    def g_at(owner, target_chip):
        return pl.ds(p * lax.rem(owner - 2 * target_chip + n, n), p)

    def a_at(owner, target):
        slot = lax.rem(owner - 2 * lax.div(target, 2) - target + 2 * n, n)
        return pl.ds(p * slot, p)

    def copy(src, dst, ss, rs, rot, az):
        return pltpu.make_async_remote_copy(
            src_ref=src, dst_ref=dst, send_sem=ss, recv_sem=rs,
            device_id={"rot": rot, "az": az}, device_id_type=pl.DeviceIdType.MESH,
        )

    lower = z < m // 2
    near_pos = jnp.where(lower, z, m - 1 - z)
    nearest = [sorted((c for c in range(m) if c != v), key=lambda c: (abs(c - v), c)) for v in range(m // 2)]

    def other(k):
        c = nearest[0][k]
        for v in range(1, m // 2):
            c = jnp.where(near_pos == v, nearest[v][k], c)
        return jnp.where(lower, c, m - 1 - c)

    loads = [
        [
            pltpu.make_async_copy(
                filt.at[s, i, j],
                weights.at[l, pl.ds(s * C, C), pl.ds((i * 3 + j) * C, C)],
                w_sem.at[l, (s * 3 + i) * 3 + j],
            )
            for s in range(p) for i in range(3) for j in range(3)
        ]
        for l, filt in enumerate((filt_two, filt_one))
    ]
    fetch = [
        pltpu.make_async_copy(a, b, v_sem.at[k])
        for k, (a, b) in enumerate(
            ((cot_at, cot), (pre_two_at, pre_two), (pre_one_at, pre_one), (inputs_at, inputs),
             (inputs_at, field_in.at[a_at(me, me), z]))
        )
    ]
    for load in fetch + loads[0] + loads[1]:
        load.start()

    barrier = pltpu.get_barrier_semaphore()
    near_cols = sorted({1 % m, (m - 1) % m})
    partners = [(sib, z)] + [(to(t), z) for t in range(1, nc)]
    partners += [(to(t), col(d)) for d in near_cols for t in range(nc)]
    partners += [(me, col(d)) for d in range(1, m) if d not in near_cols]
    for rot, az in partners:
        pl.semaphore_signal(
            barrier, inc=1, device_id={"rot": rot, "az": az},
            device_id_type=pl.DeviceIdType.MESH,
        )

    pending = []
    def start(c):
        c.start()
        pending.append(c)
        return c

    def stage_grad(ph, value):
        st_g[ph] = value.astype(BF16)
        if ph == 0:
            grads[me] = value.astype(BF16)
        else:
            whole_g[g_at(me, chip), z, 1 : H + 1] = value.astype(BF16)
        st_e[ph, 0] = value[:, :, 0, :].reshape(p * H, C).astype(BF16)
        st_e[ph, 1] = value[:, :, X - 1, :].reshape(p * H, C).astype(BF16)

    def home(ph, owner, target_chip, zz):
        if ph == 0:
            return grads.at[owner]
        return whole_g.at[g_at(owner, target_chip), zz, pl.ds(1, H)]

    def there(t):
        return lax.rem(chip + t, nc)

    def send_grad(ph):
        rims = []
        for t in range(nc):
            for side, d in ((1, 1), (0, m - 1)):
                rims.append(
                    start(
                        copy(
                            st_e.at[ph, side], edges.at[ph, me, 1 - side],
                            e_ss.at[ph, side, t], e_rs.at[ph, side, t], to(t), col(d),
                        )
                    )
                )
        direct = [None] + [
            start(copy(st_g.at[ph], home(ph, me, there(t), z), g_ss.at[ph, t], g_rs.at[ph, t], to(t), z))
            for t in range(1, nc)
        ]
        own = start(copy(st_g.at[ph], home(ph, me, chip, z), gf_ss.at[ph, 0], gf_rs.at[ph, 0], sib, z))
        return direct, own, rims

    def relay_grad(ph, sent):
        direct, own, rims = sent
        passed = [own]
        for t in range(nc):
            rims[2 * t].wait_recv()
            rims[2 * t + 1].wait_recv()
            d = frm(t)
            passed.append(
                start(copy(edges.at[ph, d], edges.at[ph, d], ef_ss.at[ph, t], ef_rs.at[ph, t], sib, z))
            )
        for t in range(1, nc):
            direct[t].wait_recv()
            d = frm(t)
            passed.append(
                start(copy(home(ph, d, chip, z), home(ph, d, chip, z), gf_ss.at[ph, t], gf_rs.at[ph, t], sib, z))
            )
        return passed

    def stage_feat(value):
        for o in range(p):
            turned = value[o].T.astype(BF16)
            st_a[o] = turned
            feats[me, o] = turned

    def send_feat():
        direct = [None] + [
            start(copy(st_a, feats.at[me], a_ss.at[0, t], a_rs.at[0, t], to(t), z))
            for t in range(1, nc)
        ]
        own = start(copy(st_a, feats.at[me], af_ss.at[0, 0], af_rs.at[0, 0], sib, z))
        return direct, own

    def relay_feat(sent):
        direct, own = sent
        passed = [own]
        for t in range(1, nc):
            direct[t].wait_recv()
            d = frm(t)
            passed.append(
                start(copy(feats.at[d], feats.at[d], af_ss.at[0, t], af_rs.at[0, t], sib, z))
            )
        return passed

    def source(f):
        return st_g.at[1] if f else inputs

    def place(f, owner, target, zz):
        if f:
            return home(1, owner, lax.div(target, 2), zz)
        return field_in.at[a_at(owner, target), zz]

    def send_cols(f):
        return [
            start(copy(source(f), place(f, me, me, z), cz_ss.at[f, k], cz_rs.at[f, z], me, other(k)))
            for k in range(m - 1)
        ]

    def spread_at(f, k, zz, src):
        passed = [start(copy(src, place(f, me, sib, zz), hf_ss.at[f, k, 0], hf_rs.at[f, k, 0], sib, z))]
        direct = [None] + [
            start(copy(src, place(f, me, to(t), zz), h_ss.at[f, k, t], h_rs.at[f, k, t], to(t), z))
            for t in range(1, nc)
        ]
        return zz, passed, direct

    def spread_col(f, k):
        zz = other(k)
        here = place(f, me, me, zz)
        copy(here, here, cz_ss.at[f, k], cz_rs.at[f, zz], me, zz).wait_recv()
        return spread_at(f, k, zz, here)

    def relay_cols(f, k, forward):
        zz, passed, direct = forward
        for t in range(1, nc):
            direct[t].wait_recv()
            d = frm(t)
            passed.append(
                start(
                    copy(place(f, d, me, zz), place(f, d, sib, zz), hf_ss.at[f, k, t], hf_rs.at[f, k, t], sib, z)
                )
            )

    def turn_col(zz):
        x_of = lax.broadcasted_iota(jnp.int32, (H, X, C), 1).reshape(HX, C)
        many = 4 if R % 4 == 0 else 1

        def rim(v, c, x):
            edge = field_in[v, c].astype(F32)[:, x, :]
            return jnp.broadcast_to(edge[:, None, :], (H, X, C)).reshape(HX, C)

        def body(b, carry):
            for u in range(many):
                v = b * many + u
                at = pl.ds(pl.multiple_of((zz * R + v) * HX, HX), HX)
                a = field_in[v, zz].reshape(HX, C)
                wide = a.astype(F32)
                low = rim(v, lax.rem(zz + m - 1, m), X - 1)
                high = rim(v, lax.rem(zz + 1, m), 0)
                before = jnp.where(x_of == 0, low, pltpu.roll(wide, 1, 0))
                after = jnp.where(x_of == X - 1, high, pltpu.roll(wide, HX - 1, 0))
                whole_in[0:C, at] = before.astype(BF16).T
                whole_in[C : 2 * C, at] = a.T
                whole_in[2 * C : 3 * C, at] = after.astype(BF16).T
            return carry

        lax.fori_loop(0, R // many, body, 0)

    def column(step):
        if m != 4:
            return step
        return z if step == 0 else other(step - 1)

    def col_terms(step):
        zz = column(step)
        for i in range(3):
            left = whole_in[:, pl.ds(pl.multiple_of(zz * R * HX, R * HX), R * HX)]
            sides = []
            for s in range(p):
                rows = [whole_g[R - s : R, zz, 2 - i : 2 - i + H].reshape(s * HX, C)] if s else []
                rows.append(whole_g[0 : R - s, zz, 2 - i : 2 - i + H].reshape((R - s) * HX, C))
                sides.append(jnp.concatenate(rows, axis=0))
            got = jnp.dot(left, jnp.concatenate(sides, axis=1), preferred_element_type=F32)
            if step == m - 1:
                if m == 4:
                    got = got + acc[1, i]
                got = got + acc[0, i]
                for s in range(p):
                    for j in range(3):
                        out_f1[(s * 3 + i) * 3 + j] = got[j * C : (j + 1) * C, s * C : (s + 1) * C].astype(BF16)
            elif step == 0 or (m == 4 and step == 2):
                acc[step // 2, i] = got
            else:
                acc[0, i] = acc[0, i] + got

    def arrive(copies):
        for c in copies:
            c.wait_recv()

    def build_gx(ph):
        x_of = lax.broadcasted_iota(jnp.int32, (p * H, X, C), 1).reshape(p * HX, C)

        def body(d, carry):
            g = grads[d] if ph == 0 else whole_g[g_at(d, chip), z, 1 : H + 1]
            g = g.astype(F32).reshape(p * HX, C)
            low = edges[ph, d, 0].astype(F32)
            high = edges[ph, d, 1].astype(F32)
            low = jnp.broadcast_to(low[:, None, :], (p * H, X, C)).reshape(p * HX, C)
            high = jnp.broadcast_to(high[:, None, :], (p * H, X, C)).reshape(p * HX, C)
            before = jnp.where(x_of == 0, low, pltpu.roll(g, 1, 0))
            after = jnp.where(x_of == X - 1, high, pltpu.roll(g, p * HX - 1, 0))
            for j, v in enumerate((after, g, before)):
                gx[pl.ds(d * p, p), 1 : H + 1, :, j * C : (j + 1) * C] = v.astype(BF16).reshape(p, H, X, C)
            return carry

        lax.fori_loop(0, n, body, 0)

    def build_lhs():
        lane = lax.broadcasted_iota(jnp.int32, (C, HX), 1)
        for q in range(n):
            owner = lax.rem(me + q, n)
            for o in range(p):
                block = q * p + o
                a = feats[owner, o]
                wide = a.astype(F32)
                down = jnp.where(lane < X, 0.0, pltpu.roll(wide, X, 1)).astype(BF16)
                up = jnp.where(lane >= HX - X, 0.0, pltpu.roll(wide, HX - X, 1)).astype(BF16)
                spots = [block] + ([R + block] if block < p - 1 else [])
                for spot in spots:
                    for i, v in enumerate((down, a, up)):
                        lhs[i * C : (i + 1) * C, spot * HX : (spot + 1) * HX] = v

    def term(q, o):
        total = None
        for s in range(p):
            one = outs[(q * p + o - s) % R, :, s * C : (s + 1) * C]
            total = one if total is None else total + one
        return total

    def data_terms(ph, beside):
        for load in loads[ph]:
            load.wait()
        w = weights[ph]
        crossed = [None] * n

        def emit(q):
            for o in range(p):
                part_s[ph, q, o] = term(q, o).astype(BF16)
            t = lax.rem(q // 2 + core, nc)
            crossed[q] = start(
                copy(part_s.at[ph, q], part_x.at[ph, t], x_ss.at[ph, t], x_rs.at[ph, t], sib, z)
            )

        for q in range(n):
            rows = jnp.concatenate(
                [gx[q * p : (q + 1) * p, 2 - i : 2 - i + H].reshape(p * HX, 3 * C) for i in range(3)],
                axis=1,
            )
            got = lax.dot_general(rows, w, (((1,), (1,)), ((), ())), preferred_element_type=F32)
            outs[q * p : (q + 1) * p] = got.reshape(p, HX, p * C)
            if q % 2 == 1:
                emit(q)
            if q in beside:
                beside[q]()

    def merge_terms(ph, ts):
        for t in ts:
            pltpu.make_async_remote_copy(
                src_ref=part_x.at[ph, t], dst_ref=part_x.at[ph, t],
                send_sem=x_ss.at[ph, t], recv_sem=x_rs.at[ph, t],
                device_id={"rot": sib, "az": z}, device_id_type=pl.DeviceIdType.MESH,
            ).wait_recv()
            for o in range(p):
                total = term(2 * t, o) + part_x[ph, t, o].astype(F32)
                if t == 0:
                    part_r[ph, 0, o] = total.astype(BF16)
                else:
                    part_m[ph, t, o] = total.astype(BF16)
            if t > 0:
                merged[ph].append(
                    start(
                        copy(part_m.at[ph, t], part_r.at[ph, t], p_ss.at[ph, t], p_rs.at[ph, t], to(t), z)
                    )
                )

    merged = ([], [])

    def part_sum(ph, copies):
        arrive(copies)
        total = part_r[ph, 0].astype(F32)
        for t in range(1, nc):
            total = total + part_r[ph, t].astype(F32)
        return total

    right, left = jnp.minimum(z + 1, m - 1), jnp.maximum(z - 1, 0)
    inner = jnp.where(lower, right, left)
    outer = jnp.where(lower, left, right)
    at_end = near_pos == 0
    at_mid = near_pos == m // 2 - 1
    slot = jnp.where(at_mid, 1, 0)

    def inward(src, k):
        return copy(src, zr.at[slot, k], z_ss.at[k], z_rs.at[slot, k], me, inner)

    def crossed_in(w, k):
        return copy(zr.at[w, k], zr.at[w, k], z_ss.at[k], z_rs.at[w, k], me, inner)

    def outward(k):
        return copy(out_f2.at[k], out_f2.at[k], y_ss.at[k], y_rs.at[k], me, outer)

    def filt_terms():
        right_side = gx[:, 1 : H + 1].reshape(R * HX, 3 * C)
        for s in range(p):
            got = jnp.dot(
                lhs[:, s * HX : (s + R) * HX], right_side, preferred_element_type=F32
            )
            for i in range(3):
                for j in range(3):
                    zs[(s * 3 + i) * 3 + j] = got[i * C : (i + 1) * C, j * C : (j + 1) * C].astype(BF16)
            if s == 0:
                begin(0, min(7, 18 // p))

    def begin(a, b):
        @pl.when(at_end)
        def _():
            for k in range(K * a // 18, K * b // 18):
                inward(zs.at[k], k).start()

    def go_in(a, b):
        @pl.when(jnp.logical_not(at_end))
        def _():
            for k in range(K * a // 18, K * b // 18):
                crossed_in(0, k).wait_recv()
                zt[k] = (zs[k].astype(F32) + zr[0, k].astype(F32)).astype(BF16)
                inward(zt.at[k], k).start()

    base = zs if m == 2 else zt

    def cross(a, b):
        @pl.when(at_mid)
        def _():
            for k in range(K * a // 18, K * b // 18):
                crossed_in(1, k).wait_recv()
                out_f2[k] = (base[k].astype(F32) + zr[1, k].astype(F32)).astype(BF16)

                @pl.when(jnp.logical_not(at_end))
                def _():
                    outward(k).start()

    def settle(a, b):
        for k in range(K * a // 18, K * b // 18):

            @pl.when(jnp.logical_not(at_mid))
            def _():
                outward(k).wait_recv()

                @pl.when(jnp.logical_not(at_end))
                def _():
                    outward(k).start()


    def drain():
        for k in range(K):
            crossed_in(0, k).wait_send()

        @pl.when(jnp.logical_not(at_end))
        def _():
            for k in range(K):
                outward(k).wait_send()

    fetch[0].wait()
    fetch[1].wait()
    grad_two = (cot[...].astype(F32) * slope(pre_two[...].astype(F32))).astype(BF16).astype(F32)
    stage_grad(0, grad_two)
    fetch[2].wait()
    wide_one = pre_one[...].astype(F32)
    stage_feat((wide_one * jax.nn.sigmoid(wide_one)).reshape(p, HX, C))
    turn[...] = slope(wide_one)
    gx[:, 0] = jnp.zeros((R, X, 3 * C), BF16)
    gx[:, H + 1] = jnp.zeros((R, X, 3 * C), BF16)
    whole_g[:, :, 0] = jnp.zeros((R, m, X, C), BF16)
    whole_g[:, :, H + 1] = jnp.zeros((R, m, X, C), BF16)
    fetch[3].wait()
    fetch[4].wait()
    pl.semaphore_wait(barrier, len(partners))
    g_sent = send_grad(0)
    send_cols(0)
    a_sent = send_feat()
    moves = {}

    def spread(f, *ks):
        for k in ks:
            if k < m - 1:
                moves[f, k] = spread_col(f, k)

    def relay(f, *ks):
        for k in ks:
            relay_cols(f, k, moves[f, k])

    kept = {}
    g_passed = relay_grad(0, g_sent)
    spread(0, 0)
    arrive(g_passed)
    build_gx(0)
    data_terms(0, {
        n // 8: lambda: spread(0, 1),
        n // 2: lambda: kept.update(a=relay_feat(a_sent)),
        n - 2: lambda: merge_terms(0, range(1, max(1, nc // 2))),
    })
    arrive(kept["a"])
    build_lhs()
    merge_terms(0, [*range(max(1, nc // 2), nc), 0])
    spread(0, *range(2, m - 1))
    moves[0, m - 1] = spread_at(0, m - 1, z, inputs)
    filt_terms()
    relay(0, *range(min(2, m - 1)))

    delta = part_sum(0, merged[0]).reshape(p, H, X, C)
    grad_one = (delta * turn[...]).astype(BF16).astype(F32)
    stage_grad(1, grad_one)
    g_sent = send_grad(1)
    send_cols(1)
    begin(min(7, 18 // p), 18)
    relay(0, *range(2, m))
    go_in(0, 7)
    for k in range(m):
        arrive(moves[0, k][1])
    if m != 4:
        for c in range(m):
            turn_col(c)
    else:
        turn_col(column(0))
        turn_col(column(1))
    spread(1, 0)
    g_passed = relay_grad(1, g_sent)
    if m == 4:
        turn_col(column(2))
    arrive(g_passed)
    build_gx(1)
    data_terms(1, {
        n // 4: lambda: spread(1, 1),
        3 * n // 4 - 1: lambda: spread(1, *range(2, m - 1)),
        n - 2: lambda: merge_terms(1, range(1, max(1, nc // 2))),
    })
    merge_terms(1, [*range(max(1, nc // 2), nc), 0])
    cols = [moves[1, k][1] for k in range(m - 1)]
    if m == 4:
        turn_col(column(3))
        col_terms(0)
    relay(1, 0)
    go_in(7, 18)
    cross(0, 7)
    relay(1, *range(1, m - 1))
    if m == 4:
        arrive(cols[0])
        col_terms(1)
    settle(0, 7)
    cross(7, 11)
    out_in[...] = part_sum(1, merged[1]).astype(BF16).reshape(p, H, X, C)
    if m == 4:
        arrive(cols[1])
        col_terms(2)
    settle(7, 11)
    cross(11, 18)
    if m == 4:
        arrive(cols[2])
        col_terms(3)
    else:
        for passed in cols:
            arrive(passed)
        for step in range(m):
            col_terms(step)
    settle(11, 18)
    for c in pending:
        c.wait_send()
    drain()


def emit(scale, got, one, two, out, out_one, out_two, wide, sems):
    k, half = one.shape[0], one.shape[0] // 3
    moves = [pltpu.make_async_copy(got, out, sems.at[0])]
    moves[0].start()
    for f, (a, b) in enumerate(((one, out_one), (two, out_two))):
        for c in range(0, k, half):
            wide[f, c : c + half] = a[c : c + half].astype(F32) * scale
            moves.append(
                pltpu.make_async_copy(
                    wide.at[f, c : c + half], b.at[c : c + half], sems.at[1 + f * 3 + c // half]
                )
            )
            moves[-1].start()
    for c in moves:
        c.wait()


def solution(mesh):
    n, m = mesh.shape["rot"], mesh.shape["az"]

    def shards(inputs, pre_one, pre_two, cot, filt_one, filt_two):
        p, H, X, C = inputs.shape
        R, HX, K, nc = n * p, H * X, 9 * p, n // 2
        scale = float(R * H * X * m) ** -0.5
        dma = pltpu.SemaphoreType.DMA
        vmem = pl.BlockSpec(memory_space=pltpu.VMEM)
        anywhere = pl.BlockSpec(memory_space=pl.ANY)
        sums = jax.ShapeDtypeStruct((K, C, C), BF16)
        scratch = [
            pltpu.VMEM((p, H, X, C), BF16),
            pltpu.VMEM((p, H, X, C), BF16),
            pltpu.VMEM((p, H, X, C), BF16),
            pltpu.VMEM((p, H, X, C), BF16),
        pltpu.VMEM((2, p, H, X, C), BF16),
        pltpu.VMEM((2, 2, p * H, C), BF16),
        pltpu.VMEM((p, C, HX), BF16),
        pltpu.VMEM((n, p, H, X, C), BF16),
        pltpu.VMEM((2, n, 2, p * H, C), BF16),
        pltpu.VMEM((n, p, C, HX), BF16),
        pltpu.VMEM((2, p * C, 9 * C), BF16),
        pltpu.VMEM((R, H + 2, X, 3 * C), BF16),
        pltpu.VMEM((3 * C, (R + p - 1) * HX), BF16),
        pltpu.VMEM((R, HX, p * C), F32),
        pltpu.VMEM((2, n, p, HX, C), BF16),
        pltpu.VMEM((2, nc, p, HX, C), BF16),
        pltpu.VMEM((2, nc, p, HX, C), BF16),
        pltpu.VMEM((2, nc, p, HX, C), BF16),
        pltpu.VMEM((K, C, C), BF16),
        pltpu.VMEM((2, K, C, C), BF16),
        pltpu.VMEM((K, C, C), BF16),
        pltpu.VMEM((R, m, H, X, C), BF16),
        pltpu.VMEM((3 * C, m * R * HX), BF16),
        pltpu.VMEM((R, m, H + 2, X, C), BF16),
        pltpu.VMEM((2, 3, 3 * C, p * C), F32),
        pltpu.VMEM((p, H, X, C), F32),
        ]
        held = sum(math.prod(v.shape) * jnp.dtype(v.dtype).itemsize for v in scratch)
        held += 2 * inputs.size + 2 * 2 * K * C * C
        made = pl.pallas_call(
            functools.partial(kernel, n, m, p, H, X, C),
            out_shape=(jax.ShapeDtypeStruct((p, H, X, C), BF16), sums, sums),
            in_specs=[pl.BlockSpec(memory_space=pltpu.HBM)] * 6,
            out_specs=(vmem,) * 3,
            scratch_shapes=scratch
            + [dma((2, nc))] * 4
            + [dma((2, 2, nc))] * 2
            + [dma((2, nc))] * 2
            + [dma((2, nc))] * 8
            + [dma((K,)), dma((2, K)), dma((K,)), dma((K,))]
            + [dma((2, K)), dma((5,))]
            + [dma((2, m))] * 2
            + [dma((2, m, nc))] * 4,
            compiler_params=pltpu.CompilerParams(
                collective_id=0, has_side_effects=True, vmem_limit_bytes=held + 3 * 1024 * 1024
            ),
        )(*(pltpu.with_memory_space_constraint(v, pltpu.HBM) for v in (inputs, pre_one, pre_two, cot, filt_one, filt_two)))
        got, one, two = pl.pallas_call(
            functools.partial(emit, scale),
            out_shape=(
                jax.ShapeDtypeStruct((p, H, X, C), BF16),
                jax.ShapeDtypeStruct((K, C, C), F32),
                jax.ShapeDtypeStruct((K, C, C), F32),
            ),
            in_specs=[vmem] * 3,
            out_specs=(anywhere,) * 3,
            scratch_shapes=[pltpu.VMEM((2, K, C, C), F32), dma((7,))],
            compiler_params=pltpu.CompilerParams(vmem_limit_bytes=8 * 1024 * 1024),
        )(*made)
        return got, one.reshape(p, 3, 3, C, C), two.reshape(p, 3, 3, C, C)

    cells = P("rot", None, "az", None)
    banks = P("rot", None, None, None, None)
    return jax.shard_map(
        shards, mesh=mesh,
        in_specs=(cells,) * 4 + (banks,) * 2,
        out_specs=(cells, banks, banks),
        check_vma=False,
    )
```

```python
import functools
import math

import jax
import jax.numpy as jnp
from jax import lax
from jax.experimental import pallas as pl
from jax.experimental.pallas import tpu as pltpu
from jax.sharding import PartitionSpec as P

F32 = jnp.float32
BF16 = jnp.bfloat16


def slope(v):
    s = jax.nn.sigmoid(v)
    return s * (1.0 + v * (1.0 - s))


def kernel(
    n, m, p, H, X, C,
    inputs_at, pre_one_at, pre_two_at, cot_at, filt_one, filt_two,
    out_in, out_f1, out_f2,
    inputs, pre_one, pre_two, cot,
    st_g, st_e, st_a, grads, edges, feats, weights, gx, lhs, outs,
    part_s, part_x, part_m, part_r, zs, zr, zt,
    field_in, whole_in, whole_g, acc, turn,
    g_ss, g_rs, gf_ss, gf_rs, e_ss, e_rs, ef_ss, ef_rs, a_ss, a_rs, af_ss, af_rs,
    x_ss, x_rs, p_ss, p_rs, z_ss, z_rs, y_ss, y_rs,
    w_sem, v_sem, cz_ss, cz_rs, h_ss, h_rs, hf_ss, hf_rs,
):
    R = n * p
    HX = H * X
    nc = n // 2
    K = 9 * p
    me = lax.axis_index("rot")
    z = lax.axis_index("az")
    core = lax.rem(me, 2)
    chip = lax.div(me, 2)
    sib = me + 1 - 2 * core

    def to(t):
        return 2 * lax.rem(chip + t, nc) + core

    def frm(t):
        return 2 * lax.rem(chip + nc - t, nc) + core

    def col(d):
        return lax.rem(z + d, m)

    def g_at(owner, target_chip):
        return pl.ds(p * lax.rem(owner - 2 * target_chip + n, n), p)

    def a_at(owner, target):
        slot = lax.rem(owner - 2 * lax.div(target, 2) - target + 2 * n, n)
        return pl.ds(p * slot, p)

    def copy(src, dst, ss, rs, rot, az):
        return pltpu.make_async_remote_copy(
            src_ref=src, dst_ref=dst, send_sem=ss, recv_sem=rs,
            device_id={"rot": rot, "az": az}, device_id_type=pl.DeviceIdType.MESH,
        )

    lower = z < m // 2
    near_pos = jnp.where(lower, z, m - 1 - z)
    nearest = [sorted((c for c in range(m) if c != v), key=lambda c: (abs(c - v), c)) for v in range(m // 2)]

    def other(k):
        c = nearest[0][k]
        for v in range(1, m // 2):
            c = jnp.where(near_pos == v, nearest[v][k], c)
        return jnp.where(lower, c, m - 1 - c)

    loads = [
        [
            pltpu.make_async_copy(
                filt.at[s, i, j],
                weights.at[l, pl.ds(s * C, C), pl.ds((i * 3 + j) * C, C)],
                w_sem.at[l, (s * 3 + i) * 3 + j],
            )
            for s in range(p) for i in range(3) for j in range(3)
        ]
        for l, filt in enumerate((filt_two, filt_one))
    ]
    fetch = [
        pltpu.make_async_copy(a, b, v_sem.at[k])
        for k, (a, b) in enumerate(
            ((cot_at, cot), (pre_two_at, pre_two), (pre_one_at, pre_one), (inputs_at, inputs),
             (inputs_at, field_in.at[a_at(me, me), z]))
        )
    ]
    barrier = pltpu.get_barrier_semaphore()
    near_cols = sorted({1 % m, (m - 1) % m})
    partners = [(sib, z)] + [(to(t), z) for t in range(1, nc)]
    partners += [(to(t), col(d)) for d in near_cols for t in range(nc)]
    partners += [(me, col(d)) for d in range(1, m) if d not in near_cols]
    for rot, az in partners:
        pl.semaphore_signal(
            barrier, inc=1, device_id={"rot": rot, "az": az},
            device_id_type=pl.DeviceIdType.MESH,
        )
    for load in fetch + loads[0] + loads[1]:
        load.start()

    pending = []
    def start(c):
        c.start()
        pending.append(c)
        return c

    def stage_grad(ph, value):
        st_g[ph] = value.astype(BF16)
        if ph == 0:
            grads[me] = value.astype(BF16)
        else:
            whole_g[g_at(me, chip), z, 1 : H + 1] = value.astype(BF16)
        st_e[ph, 0] = value[:, :, 0, :].reshape(p * H, C).astype(BF16)
        st_e[ph, 1] = value[:, :, X - 1, :].reshape(p * H, C).astype(BF16)

    def home(ph, owner, target_chip, zz):
        if ph == 0:
            return grads.at[owner]
        return whole_g.at[g_at(owner, target_chip), zz, pl.ds(1, H)]

    def there(t):
        return lax.rem(chip + t, nc)

    def send_grad(ph):
        rims = []
        for t in range(nc):
            for side, d in ((1, 1), (0, m - 1)):
                rims.append(
                    start(
                        copy(
                            st_e.at[ph, side], edges.at[ph, me, 1 - side],
                            e_ss.at[ph, side, t], e_rs.at[ph, side, t], to(t), col(d),
                        )
                    )
                )
        direct = [None] + [
            start(copy(st_g.at[ph], home(ph, me, there(t), z), g_ss.at[ph, t], g_rs.at[ph, t], to(t), z))
            for t in range(1, nc)
        ]
        own = start(copy(st_g.at[ph], home(ph, me, chip, z), gf_ss.at[ph, 0], gf_rs.at[ph, 0], sib, z))
        return direct, own, rims

    def relay_grad(ph, sent):
        direct, own, rims = sent
        passed = [own]
        for t in range(nc):
            rims[2 * t].wait_recv()
            rims[2 * t + 1].wait_recv()
            d = frm(t)
            passed.append(
                start(copy(edges.at[ph, d], edges.at[ph, d], ef_ss.at[ph, t], ef_rs.at[ph, t], sib, z))
            )
        for t in range(1, nc):
            direct[t].wait_recv()
            d = frm(t)
            passed.append(
                start(copy(home(ph, d, chip, z), home(ph, d, chip, z), gf_ss.at[ph, t], gf_rs.at[ph, t], sib, z))
            )
        return passed

    def stage_feat(value):
        for o in range(p):
            turned = value[o].T.astype(BF16)
            st_a[o] = turned
            feats[me, o] = turned

    def send_feat():
        direct = [None] + [
            start(copy(st_a, feats.at[me], a_ss.at[0, t], a_rs.at[0, t], to(t), z))
            for t in range(1, nc)
        ]
        own = start(copy(st_a, feats.at[me], af_ss.at[0, 0], af_rs.at[0, 0], sib, z))
        return direct, own

    def relay_feat(sent):
        direct, own = sent
        passed = [own]
        for t in range(1, nc):
            direct[t].wait_recv()
            d = frm(t)
            passed.append(
                start(copy(feats.at[d], feats.at[d], af_ss.at[0, t], af_rs.at[0, t], sib, z))
            )
        return passed

    def source(f):
        return st_g.at[1] if f else inputs

    def place(f, owner, target, zz):
        if f:
            return home(1, owner, lax.div(target, 2), zz)
        return field_in.at[a_at(owner, target), zz]

    def send_cols(f):
        return [
            start(copy(source(f), place(f, me, me, z), cz_ss.at[f, k], cz_rs.at[f, z], me, other(k)))
            for k in range(m - 1)
        ]

    def spread_at(f, k, zz, src):
        passed = [start(copy(src, place(f, me, sib, zz), hf_ss.at[f, k, 0], hf_rs.at[f, k, 0], sib, z))]
        direct = [None] + [
            start(copy(src, place(f, me, to(t), zz), h_ss.at[f, k, t], h_rs.at[f, k, t], to(t), z))
            for t in range(1, nc)
        ]
        return zz, passed, direct

    def spread_col(f, k):
        zz = other(k)
        here = place(f, me, me, zz)
        copy(here, here, cz_ss.at[f, k], cz_rs.at[f, zz], me, zz).wait_recv()
        return spread_at(f, k, zz, here)

    def relay_cols(f, k, forward):
        zz, passed, direct = forward
        for t in range(1, nc):
            direct[t].wait_recv()
            d = frm(t)
            passed.append(
                start(
                    copy(place(f, d, me, zz), place(f, d, sib, zz), hf_ss.at[f, k, t], hf_rs.at[f, k, t], sib, z)
                )
            )

    def turn_col(zz):
        x_of = lax.broadcasted_iota(jnp.int32, (H, X, C), 1).reshape(HX, C)
        many = 4 if R % 4 == 0 else 1

        def rim(v, c, x):
            edge = field_in[v, c].astype(F32)[:, x, :]
            return jnp.broadcast_to(edge[:, None, :], (H, X, C)).reshape(HX, C)

        def body(b, carry):
            for u in range(many):
                v = b * many + u
                at = pl.ds(pl.multiple_of((zz * R + v) * HX, HX), HX)
                a = field_in[v, zz].reshape(HX, C)
                wide = a.astype(F32)
                low = rim(v, lax.rem(zz + m - 1, m), X - 1)
                high = rim(v, lax.rem(zz + 1, m), 0)
                before = jnp.where(x_of == 0, low, pltpu.roll(wide, 1, 0))
                after = jnp.where(x_of == X - 1, high, pltpu.roll(wide, HX - 1, 0))
                whole_in[0:C, at] = before.astype(BF16).T
                whole_in[C : 2 * C, at] = a.T
                whole_in[2 * C : 3 * C, at] = after.astype(BF16).T
            return carry

        lax.fori_loop(0, R // many, body, 0)

    def column(step):
        if m != 4:
            return step
        return z if step == 0 else other(step - 1)

    def col_terms(step):
        zz = column(step)
        for i in range(3):
            left = whole_in[:, pl.ds(pl.multiple_of(zz * R * HX, R * HX), R * HX)]
            sides = []
            for s in range(p):
                rows = [whole_g[R - s : R, zz, 2 - i : 2 - i + H].reshape(s * HX, C)] if s else []
                rows.append(whole_g[0 : R - s, zz, 2 - i : 2 - i + H].reshape((R - s) * HX, C))
                sides.append(jnp.concatenate(rows, axis=0))
            got = jnp.dot(left, jnp.concatenate(sides, axis=1), preferred_element_type=F32)
            if step == m - 1:
                if m == 4:
                    got = got + acc[1, i]
                got = got + acc[0, i]
                for s in range(p):
                    for j in range(3):
                        out_f1[(s * 3 + i) * 3 + j] = got[j * C : (j + 1) * C, s * C : (s + 1) * C].astype(BF16)
            elif step == 0 or (m == 4 and step == 2):
                acc[step // 2, i] = got
            else:
                acc[0, i] = acc[0, i] + got

    def arrive(copies):
        for c in copies:
            c.wait_recv()

    def build_gx(ph):
        x_of = lax.broadcasted_iota(jnp.int32, (p * H, X, C), 1).reshape(p * HX, C)

        def body(d, carry):
            g = grads[d] if ph == 0 else whole_g[g_at(d, chip), z, 1 : H + 1]
            g = g.astype(F32).reshape(p * HX, C)
            low = edges[ph, d, 0].astype(F32)
            high = edges[ph, d, 1].astype(F32)
            low = jnp.broadcast_to(low[:, None, :], (p * H, X, C)).reshape(p * HX, C)
            high = jnp.broadcast_to(high[:, None, :], (p * H, X, C)).reshape(p * HX, C)
            before = jnp.where(x_of == 0, low, pltpu.roll(g, 1, 0))
            after = jnp.where(x_of == X - 1, high, pltpu.roll(g, p * HX - 1, 0))
            for j, v in enumerate((after, g, before)):
                gx[pl.ds(d * p, p), 1 : H + 1, :, j * C : (j + 1) * C] = v.astype(BF16).reshape(p, H, X, C)
            return carry

        lax.fori_loop(0, n, body, 0)

    def build_lhs():
        lane = lax.broadcasted_iota(jnp.int32, (C, HX), 1)
        for q in range(n):
            owner = lax.rem(me + q, n)
            for o in range(p):
                block = q * p + o
                a = feats[owner, o]
                wide = a.astype(F32)
                down = jnp.where(lane < X, 0.0, pltpu.roll(wide, X, 1)).astype(BF16)
                up = jnp.where(lane >= HX - X, 0.0, pltpu.roll(wide, HX - X, 1)).astype(BF16)
                spots = [block] + ([R + block] if block < p - 1 else [])
                for spot in spots:
                    for i, v in enumerate((down, a, up)):
                        lhs[i * C : (i + 1) * C, spot * HX : (spot + 1) * HX] = v

    def term(q, o):
        total = None
        for s in range(p):
            one = outs[(q * p + o - s) % R, :, s * C : (s + 1) * C]
            total = one if total is None else total + one
        return total

    def data_terms(ph, beside):
        for load in loads[ph]:
            load.wait()
        w = weights[ph]
        crossed = [None] * n

        def emit(q):
            for o in range(p):
                part_s[ph, q, o] = term(q, o).astype(BF16)
            t = lax.rem(q // 2 + core, nc)
            crossed[q] = start(
                copy(part_s.at[ph, q], part_x.at[ph, t], x_ss.at[ph, t], x_rs.at[ph, t], sib, z)
            )

        for q in range(n):
            rows = jnp.concatenate(
                [gx[q * p : (q + 1) * p, 2 - i : 2 - i + H].reshape(p * HX, 3 * C) for i in range(3)],
                axis=1,
            )
            got = lax.dot_general(rows, w, (((1,), (1,)), ((), ())), preferred_element_type=F32)
            outs[q * p : (q + 1) * p] = got.reshape(p, HX, p * C)
            if q % 2 == 1:
                emit(q)
            if q in beside:
                beside[q]()

    def merge_terms(ph, ts):
        for t in ts:
            pltpu.make_async_remote_copy(
                src_ref=part_x.at[ph, t], dst_ref=part_x.at[ph, t],
                send_sem=x_ss.at[ph, t], recv_sem=x_rs.at[ph, t],
                device_id={"rot": sib, "az": z}, device_id_type=pl.DeviceIdType.MESH,
            ).wait_recv()
            for o in range(p):
                total = term(2 * t, o) + part_x[ph, t, o].astype(F32)
                if t == 0:
                    part_r[ph, 0, o] = total.astype(BF16)
                else:
                    part_m[ph, t, o] = total.astype(BF16)
            if t > 0:
                merged[ph].append(
                    start(
                        copy(part_m.at[ph, t], part_r.at[ph, t], p_ss.at[ph, t], p_rs.at[ph, t], to(t), z)
                    )
                )

    merged = ([], [])

    def part_sum(ph, copies):
        arrive(copies)
        total = part_r[ph, 0].astype(F32)
        for t in range(1, nc):
            total = total + part_r[ph, t].astype(F32)
        return total

    right, left = jnp.minimum(z + 1, m - 1), jnp.maximum(z - 1, 0)
    inner = jnp.where(lower, right, left)
    outer = jnp.where(lower, left, right)
    at_end = near_pos == 0
    at_mid = near_pos == m // 2 - 1
    slot = jnp.where(at_mid, 1, 0)

    def inward(src, k):
        return copy(src, zr.at[slot, k], z_ss.at[k], z_rs.at[slot, k], me, inner)

    def crossed_in(w, k):
        return copy(zr.at[w, k], zr.at[w, k], z_ss.at[k], z_rs.at[w, k], me, inner)

    def outward(k):
        return copy(out_f2.at[k], out_f2.at[k], y_ss.at[k], y_rs.at[k], me, outer)

    def filt_terms():
        right_side = gx[:, 1 : H + 1].reshape(R * HX, 3 * C)
        for s in range(p):
            got = jnp.dot(
                lhs[:, s * HX : (s + R) * HX], right_side, preferred_element_type=F32
            )
            for i in range(3):
                for j in range(3):
                    zs[(s * 3 + i) * 3 + j] = got[i * C : (i + 1) * C, j * C : (j + 1) * C].astype(BF16)
            if s == 0:
                begin(0, min(7, 18 // p))

    def begin(a, b):
        @pl.when(at_end)
        def _():
            for k in range(K * a // 18, K * b // 18):
                inward(zs.at[k], k).start()

    def go_in(a, b):
        @pl.when(jnp.logical_not(at_end))
        def _():
            for k in range(K * a // 18, K * b // 18):
                crossed_in(0, k).wait_recv()
                zt[k] = (zs[k].astype(F32) + zr[0, k].astype(F32)).astype(BF16)
                inward(zt.at[k], k).start()

    base = zs if m == 2 else zt

    def cross(a, b):
        @pl.when(at_mid)
        def _():
            for k in range(K * a // 18, K * b // 18):
                crossed_in(1, k).wait_recv()
                out_f2[k] = (base[k].astype(F32) + zr[1, k].astype(F32)).astype(BF16)

                @pl.when(jnp.logical_not(at_end))
                def _():
                    outward(k).start()

    def settle(a, b):
        for k in range(K * a // 18, K * b // 18):

            @pl.when(jnp.logical_not(at_mid))
            def _():
                outward(k).wait_recv()

                @pl.when(jnp.logical_not(at_end))
                def _():
                    outward(k).start()


    def drain():
        for k in range(K):
            crossed_in(0, k).wait_send()

        @pl.when(jnp.logical_not(at_end))
        def _():
            for k in range(K):
                outward(k).wait_send()

    fetch[0].wait()
    fetch[1].wait()
    grad_two = (cot[...].astype(F32) * slope(pre_two[...].astype(F32))).astype(BF16).astype(F32)
    stage_grad(0, grad_two)
    fetch[2].wait()
    wide_one = pre_one[...].astype(F32)
    stage_feat((wide_one * jax.nn.sigmoid(wide_one)).reshape(p, HX, C))
    turn[...] = slope(wide_one)
    gx[:, 0] = jnp.zeros((R, X, 3 * C), BF16)
    gx[:, H + 1] = jnp.zeros((R, X, 3 * C), BF16)
    whole_g[:, :, 0] = jnp.zeros((R, m, X, C), BF16)
    whole_g[:, :, H + 1] = jnp.zeros((R, m, X, C), BF16)
    fetch[3].wait()
    fetch[4].wait()
    pl.semaphore_wait(barrier, len(partners))
    g_sent = send_grad(0)
    send_cols(0)
    a_sent = send_feat()
    moves = {}

    def spread(f, *ks):
        for k in ks:
            if k < m - 1:
                moves[f, k] = spread_col(f, k)

    def relay(f, *ks):
        for k in ks:
            relay_cols(f, k, moves[f, k])

    kept = {}
    g_passed = relay_grad(0, g_sent)
    spread(0, 0)
    arrive(g_passed)
    build_gx(0)
    data_terms(0, {
        n // 8: lambda: spread(0, 1),
        n // 2: lambda: kept.update(a=relay_feat(a_sent)),
        n - 2: lambda: merge_terms(0, range(1, max(1, nc // 2))),
    })
    arrive(kept["a"])
    build_lhs()
    merge_terms(0, [*range(max(1, nc // 2), nc), 0])
    spread(0, *range(2, m - 1))
    moves[0, m - 1] = spread_at(0, m - 1, z, inputs)
    filt_terms()
    relay(0, *range(min(2, m - 1)))

    delta = part_sum(0, merged[0]).reshape(p, H, X, C)
    grad_one = (delta * turn[...]).astype(BF16).astype(F32)
    stage_grad(1, grad_one)
    g_sent = send_grad(1)
    send_cols(1)
    begin(min(7, 18 // p), 18)
    relay(0, *range(2, m))
    go_in(0, 7)
    for k in range(m):
        arrive(moves[0, k][1])
    if m != 4:
        for c in range(m):
            turn_col(c)
    else:
        turn_col(column(0))
        turn_col(column(1))
    spread(1, 0)
    g_passed = relay_grad(1, g_sent)
    if m == 4:
        turn_col(column(2))
    arrive(g_passed)
    build_gx(1)
    data_terms(1, {
        n // 4: lambda: spread(1, 1),
        3 * n // 4 - 1: lambda: spread(1, *range(2, m - 1)),
        n - 2: lambda: merge_terms(1, range(1, max(1, nc // 2))),
    })
    merge_terms(1, [*range(max(1, nc // 2), nc), 0])
    cols = [moves[1, k][1] for k in range(m - 1)]
    if m == 4:
        turn_col(column(3))
        col_terms(0)
    relay(1, 0)
    go_in(7, 18)
    cross(0, 7)
    relay(1, *range(1, m - 1))
    if m == 4:
        arrive(cols[0])
        col_terms(1)
    settle(0, 7)
    cross(7, 11)
    out_in[...] = part_sum(1, merged[1]).astype(BF16).reshape(p, H, X, C)
    if m == 4:
        arrive(cols[1])
        col_terms(2)
    settle(7, 11)
    cross(11, 18)
    if m == 4:
        arrive(cols[2])
        col_terms(3)
    else:
        for passed in cols:
            arrive(passed)
        for step in range(m):
            col_terms(step)
    settle(11, 18)
    for c in pending:
        c.wait_send()
    drain()


def emit(scale, got, one, two, out, out_one, out_two, wide, sems):
    k, half = one.shape[0], one.shape[0] // 3
    moves = [pltpu.make_async_copy(got, out, sems.at[0])]
    moves[0].start()
    for f, (a, b) in enumerate(((one, out_one), (two, out_two))):
        for c in range(0, k, half):
            wide[f, c : c + half] = a[c : c + half].astype(F32) * scale
            moves.append(
                pltpu.make_async_copy(
                    wide.at[f, c : c + half], b.at[c : c + half], sems.at[1 + f * 3 + c // half]
                )
            )
            moves[-1].start()
    for c in moves:
        c.wait()


def solution(mesh):
    n, m = mesh.shape["rot"], mesh.shape["az"]

    def shards(inputs, pre_one, pre_two, cot, filt_one, filt_two):
        p, H, X, C = inputs.shape
        R, HX, K, nc = n * p, H * X, 9 * p, n // 2
        scale = float(R * H * X * m) ** -0.5
        dma = pltpu.SemaphoreType.DMA
        vmem = pl.BlockSpec(memory_space=pltpu.VMEM)
        anywhere = pl.BlockSpec(memory_space=pl.ANY)
        sums = jax.ShapeDtypeStruct((K, C, C), BF16)
        scratch = [
            pltpu.VMEM((p, H, X, C), BF16),
            pltpu.VMEM((p, H, X, C), BF16),
            pltpu.VMEM((p, H, X, C), BF16),
            pltpu.VMEM((p, H, X, C), BF16),
        pltpu.VMEM((2, p, H, X, C), BF16),
        pltpu.VMEM((2, 2, p * H, C), BF16),
        pltpu.VMEM((p, C, HX), BF16),
        pltpu.VMEM((n, p, H, X, C), BF16),
        pltpu.VMEM((2, n, 2, p * H, C), BF16),
        pltpu.VMEM((n, p, C, HX), BF16),
        pltpu.VMEM((2, p * C, 9 * C), BF16),
        pltpu.VMEM((R, H + 2, X, 3 * C), BF16),
        pltpu.VMEM((3 * C, (R + p - 1) * HX), BF16),
        pltpu.VMEM((R, HX, p * C), F32),
        pltpu.VMEM((2, n, p, HX, C), BF16),
        pltpu.VMEM((2, nc, p, HX, C), BF16),
        pltpu.VMEM((2, nc, p, HX, C), BF16),
        pltpu.VMEM((2, nc, p, HX, C), BF16),
        pltpu.VMEM((K, C, C), BF16),
        pltpu.VMEM((2, K, C, C), BF16),
        pltpu.VMEM((K, C, C), BF16),
        pltpu.VMEM((R, m, H, X, C), BF16),
        pltpu.VMEM((3 * C, m * R * HX), BF16),
        pltpu.VMEM((R, m, H + 2, X, C), BF16),
        pltpu.VMEM((2, 3, 3 * C, p * C), F32),
        pltpu.VMEM((p, H, X, C), F32),
        ]
        held = sum(math.prod(v.shape) * jnp.dtype(v.dtype).itemsize for v in scratch)
        held += 2 * inputs.size + 2 * 2 * K * C * C
        made = pl.pallas_call(
            functools.partial(kernel, n, m, p, H, X, C),
            out_shape=(jax.ShapeDtypeStruct((p, H, X, C), BF16), sums, sums),
            in_specs=[pl.BlockSpec(memory_space=pltpu.HBM)] * 6,
            out_specs=(vmem,) * 3,
            scratch_shapes=scratch
            + [dma((2, nc))] * 4
            + [dma((2, 2, nc))] * 2
            + [dma((2, nc))] * 2
            + [dma((2, nc))] * 8
            + [dma((K,)), dma((2, K)), dma((K,)), dma((K,))]
            + [dma((2, K)), dma((5,))]
            + [dma((2, m))] * 2
            + [dma((2, m, nc))] * 4,
            compiler_params=pltpu.CompilerParams(
                collective_id=0, has_side_effects=True, vmem_limit_bytes=held + 3 * 1024 * 1024
            ),
        )(*(pltpu.with_memory_space_constraint(v, pltpu.HBM) for v in (inputs, pre_one, pre_two, cot, filt_one, filt_two)))
        got, one, two = pl.pallas_call(
            functools.partial(emit, scale),
            out_shape=(
                jax.ShapeDtypeStruct((p, H, X, C), BF16),
                jax.ShapeDtypeStruct((K, C, C), F32),
                jax.ShapeDtypeStruct((K, C, C), F32),
            ),
            in_specs=[vmem] * 3,
            out_specs=(anywhere,) * 3,
            scratch_shapes=[pltpu.VMEM((2, K, C, C), F32), dma((7,))],
            compiler_params=pltpu.CompilerParams(vmem_limit_bytes=8 * 1024 * 1024),
        )(*made)
        return got, one.reshape(p, 3, 3, C, C), two.reshape(p, 3, 3, C, C)

    cells = P("rot", None, "az", None)
    banks = P("rot", None, None, None, None)
    return jax.shard_map(
        shards, mesh=mesh,
        in_specs=(cells,) * 4 + (banks,) * 2,
        out_specs=(cells, banks, banks),
        check_vma=False,
    )
```
